32 devices in a mesh: groups: 2 (over x), weight: 16 (over z, y, core).
Axes of the slice: x: 2, y: 2, z: 4, core: 2. Of those that a mesh axis runs over, the one named last changes fastest.
Arguments:
- hidden: bfloat16 [128, 8192], P(('groups', 'weight')), parts along dimension 0, may hold values from -6 to 6
- norm_gain: float32 [8192], replicated, may hold values from 0.1 to 1.9
- in_weight: bfloat16 [8192, 2, 8192], P(None, None, 'weight'), may hold values from -0.0625 to 0.0625
- conv_weight: float32 [4, 8192], P(None, 'weight'), may hold values from -0.6 to 0.6
- conv_offset: float32 [8192], P('weight'), may hold values from -0.5 to 0.5
- coef_weight: bfloat16 [8192, 544], P('weight'), may hold values from -0.0625 to 0.0625
- step_weight: bfloat16 [512, 8192], P(None, 'weight'), may hold values from -0.25 to 0.25
- step_bias: float32 [8192], P('weight'), may hold values from -3 to 0.5
- log_rates: float32 [16, 8192], P(None, 'weight'), may hold values from 0 to 2.77
- skip_gain: float32 [8192], P('weight'), may hold values from 0.5 to 1.5
- out_weight: bfloat16 [8192, 8192], P('weight'), may hold values from -0.0625 to 0.0625
- ssm_state: bfloat16 [128, 16, 8192], P('groups', None, 'weight'), parts along dimension 0, may hold values from -6 to 6
- conv_state: bfloat16 [128, 3, 8192], P('groups', None, 'weight'), parts along dimension 0, may hold values from -6 to 6
- live_counts: int32 [32], P('groups'), parts along dimension 0, may hold values from 1 to 3, as said below
Outputs:
- mixed: bfloat16 [128, 8192], P(('groups', 'weight')), parts along dimension 0
- new_state: bfloat16 [128, 16, 8192], P('groups', None, 'weight'), parts along dimension 0
- new_conv: bfloat16 [128, 3, 8192], P('groups', None, 'weight'), parts along dimension 0
The draws below stay inside these ranges and needn't reach their ends.
There are 2 independent parts, one for each index of `groups`. The reference program is written for one: setup_inputs(seed, part) draws one part's arguments, and reference() takes and returns one part's arrays. A program takes and returns all parts, laid end to end along the dimension named above; an argument that names none is the same for every part. Nothing has to cross between parts.
Inputs may be any that keep to these rules, and one draw needn't show every extreme that they name: The live rows of a microbatch are its first live_counts rows; the most, 3, is reached by some microbatch.
All inputs are finite; a program needn't handle non-finite values.
Results may differ from the reference program's by a relative error of at most 0.0039.
Values may be sent and summed in bfloat16 or wider, within the bound.
A program may use at most 64 MiB of HBM per device.

```python
import jax
import jax.numpy as jnp
from jax import lax

D = 8192
E = 8192
NSTATE = 16
DTR = 512
ROWS_DEV = 4
LIVE_MAX = 3
MICRO = 16
R = 64


def draw_live_counts(key, part):
    base = jax.random.fold_in(key, 11)
    first_key, second_key = jax.random.split(base)
    counts = jax.random.randint(first_key, (MICRO,), 1, LIVE_MAX + 1)
    chosen = jax.random.randint(second_key, (), 0, MICRO)
    filled = jnp.where(jnp.arange(MICRO) == chosen, LIVE_MAX, counts)
    return filled.astype(jnp.int32)


def block_scale(stream_key, dims, cuts, least, high):
    factor_of, own = 1.0, jax.random.fold_in(stream_key, 6)
    for axis_at, parts in cuts:
        draws = jnp.exp(jax.random.uniform(jax.random.fold_in(own, axis_at), (parts,), jnp.float32, least / len(cuts), high / len(cuts)))
        factor_of = factor_of * jnp.repeat(draws, dims[axis_at] // parts).reshape([-1 if axis == axis_at else 1 for axis in range(len(dims))])
    return factor_of


def centred(rng, shape, scale, limit, cuts=(), kind=jnp.bfloat16):
    result = scale * jax.random.normal(rng, shape, jnp.float32)
    if cuts:
        result = result * block_scale(rng, shape, cuts, -0.22, 0.18)
    return jnp.clip(result, -limit, limit).astype(kind)


def setup_inputs(seed: int = 0, part: int = 0) -> dict:
    arg_keys = jax.random.split(jax.random.key(seed), 15)
    part_keys = jax.random.split(jax.random.fold_in(arg_keys[14], part), 15)
    hidden = centred(part_keys[0], (R, D), 1.0, 6.0, ((0, 16),))
    norm_gain = jnp.clip(1.0 + 0.18 * jax.random.normal(arg_keys[1], (D,), jnp.float32), 0.1, 1.9)
    in_weight = centred(arg_keys[2], (D, 2, E), D ** -0.5, 0.0625, ((2, 16),))
    conv_weight = jnp.clip(jax.random.uniform(arg_keys[3], (4, E), jnp.float32, -0.6, 0.6) * block_scale(arg_keys[3], (4, E), ((1, 16),), -0.4, 0.0), -0.6, 0.6)
    conv_offset = jnp.clip(jax.random.uniform(arg_keys[4], (E,), jnp.float32, -0.5, 0.5) * block_scale(arg_keys[4], (E,), ((0, 16),), -0.4, 0.0), -0.5, 0.5)
    coef_weight = centred(arg_keys[5], (E, DTR + 2 * NSTATE), E ** -0.5, 0.0625, ((0, 16),))
    step_weight = centred(arg_keys[6], (DTR, E), DTR ** -0.5, 0.25, ((1, 16),))
    step_bias = jnp.clip(-3.0 + 3.5 * jax.random.uniform(arg_keys[7], (E,), jnp.float32) ** block_scale(arg_keys[7], (E,), ((0, 16),), -0.2, 0.2), -3.0, 0.5)
    log_rates = jnp.clip(2.77 * jax.random.uniform(arg_keys[8], (NSTATE, E), jnp.float32) ** block_scale(arg_keys[8], (NSTATE, E), ((1, 16),), -0.2, 0.2), 0.0, 2.77)
    skip_gain = jnp.clip(0.5 + 1.0 * jax.random.uniform(arg_keys[9], (E,), jnp.float32) ** block_scale(arg_keys[9], (E,), ((0, 16),), -0.2, 0.2), 0.5, 1.5)
    out_weight = centred(arg_keys[10], (E, D), E ** -0.5, 0.0625, ((0, 16),))
    ssm_state = centred(part_keys[11], (R, NSTATE, E), 1.0, 6.0, ((2, 16),))
    conv_state = centred(part_keys[12], (R, 3, E), 1.0, 6.0, ((2, 16),))
    live_counts = draw_live_counts(jax.random.fold_in(jax.random.fold_in(arg_keys[14], part), 71), part)
    return {"hidden": hidden, "norm_gain": norm_gain, "in_weight": in_weight, "conv_weight": conv_weight, "conv_offset": conv_offset, "coef_weight": coef_weight, "step_weight": step_weight, "step_bias": step_bias, "log_rates": log_rates, "skip_gain": skip_gain, "out_weight": out_weight, "ssm_state": ssm_state, "conv_state": conv_state, "live_counts": live_counts}


def rms_normed(hidden, norm_gain):
    wide = hidden.astype(jnp.float32)
    factor = lax.rsqrt(lax.optimization_barrier(jnp.mean(wide * wide, axis=-1, keepdims=True)) + 1e-05)
    return (wide * factor * norm_gain).astype(jnp.bfloat16)

def reference(hidden, norm_gain, in_weight, conv_weight, conv_offset, coef_weight, step_weight, step_bias, log_rates, skip_gain, out_weight, ssm_state, conv_state, live_counts):
    total_rows = hidden.shape[0]
    row_ids = jnp.arange(total_rows, dtype=jnp.int32)
    per_row = jnp.repeat(live_counts, ROWS_DEV, total_repeat_length=total_rows)
    alive = row_ids % ROWS_DEV < per_row
    normed = rms_normed(hidden, norm_gain)
    conv_input = jnp.dot(normed, in_weight[:, 0, :], preferred_element_type=jnp.float32).astype(jnp.bfloat16)
    gate_branch = jnp.dot(normed, in_weight[:, 1, :], preferred_element_type=jnp.float32)
    window = jnp.concatenate([conv_state, conv_input[:, None, :]], axis=1)
    convolved = lax.optimization_barrier(jnp.sum(window.astype(jnp.float32) * conv_weight[None], axis=1)) + conv_offset
    mixed_x = jax.nn.silu(convolved).astype(jnp.bfloat16)
    low_rank = jnp.dot(mixed_x, coef_weight, preferred_element_type=jnp.float32)
    step_low = low_rank[:, :DTR].astype(jnp.bfloat16)
    in_coef = low_rank[:, DTR:DTR + NSTATE]
    out_coef = low_rank[:, DTR + NSTATE:]
    step_size = jax.nn.softplus(jnp.dot(step_low, step_weight, preferred_element_type=jnp.float32) + step_bias)
    x_wide = mixed_x.astype(jnp.float32)
    decays = jnp.exp(-step_size[:, None, :] * jnp.exp(log_rates)[None])
    old_state = ssm_state.astype(jnp.float32)
    updated = decays * old_state + step_size[:, None, :] * in_coef[:, :, None] * x_wide[:, None, :]
    readout = lax.optimization_barrier(jnp.sum(out_coef[:, :, None] * updated, axis=1)) + skip_gain * x_wide
    gated_out = jnp.where(alive[:, None], readout * jax.nn.silu(gate_branch), 0.0).astype(jnp.bfloat16)
    mixer_term = jnp.dot(gated_out, out_weight, preferred_element_type=jnp.float32)
    mixed = (hidden.astype(jnp.float32) + mixer_term).astype(jnp.bfloat16)
    new_state = jnp.where(alive[:, None, None], updated, old_state).astype(jnp.bfloat16)
    new_conv = jnp.where(alive[:, None, None], window[:, 1:], conv_state)
    return (mixed, new_state, new_conv)
```

```python
import functools

import jax
import jax.numpy as jnp
from jax import lax
from jax.experimental import pallas as pl
from jax.experimental.pallas import tpu as pltpu
from jax.sharding import PartitionSpec as P

NSTATE = 16
DTR = 512
LIVE_MAX = 3
LANES = 128
F32 = jnp.float32
BF16 = jnp.bfloat16
MESH = pl.DeviceIdType.MESH
KSPLIT = 8
PARTS = 4
GROUP = 16
EARLY = 4


def iota(shape, dim):
    return lax.broadcasted_iota(jnp.int32, shape, dim)


def dot(a, b):
    return jnp.dot(a, b, preferred_element_type=F32)


def kernel(
    n, lb,
    hidden, gain, convw, convo, sbias, lograte, skip, live,
    w_hbm, coef_hbm, stepw_hbm, outw_hbm, ssm_hbm, conv_hbm,
    mixed, state_out, conv_out,
    raw, perm, wd, coefv, stepv, outv, ssmv, convv, newconv,
    xs, xg, xf, lhs, acc, mx, sgate, lowp, lowf, lowr, lowg, inb, outb, step, ro, erate,
    pf, s1, r1, k1, s2, r2, k2, s3, r3, fin,
    wsem, lsem, osem, a_s, a_r, b_s, b_r, c_s, c_r, d_s, d_r, e_s, e_r, f_s, f_r, g_s, g_r, h_s, h_r,
):
    me = lax.axis_index("weight")
    core = me % 2
    y = (me // 2) % 2
    z = me // 4
    outer = n // 4
    depth = hidden.shape[1]
    rows_dev = hidden.shape[0]
    ch = depth // LANES
    cq = ch // PARTS
    part = LIVE_MAX * cq
    rows = LIVE_MAX * n
    allrows = rows_dev * n
    chan = wd.shape[2]
    tiles = chan // LANES
    kpart = depth // PARTS
    chunks = (DTR + 2 * NSTATE + LANES - 1) // LANES
    wide = DTR + 2 * NSTATE

    def at(zz, yy, cc):
        return zz * 4 + yy * 2 + cc

    def slab(yy, cc):
        return cc * (2 * outer) + yy * outer

    def device_of(s):
        return at(s % outer, (s // outer) % 2, s // (2 * outer))

    def slot_of(d):
        return slab((d // 2) % 2, d % 2) + d // 4

    ypeer = at(z, 1 - y, core)
    cpeer = at(z, y, 1 - core)
    slot = slab(y, core) + z

    def rdma(src, dst, send, recv, dev):
        return pltpu.make_async_remote_copy(
            src_ref=src, dst_ref=dst, send_sem=send, recv_sem=recv,
            device_id={"weight": dev}, device_id_type=MESH,
        )

    span = raw.shape[0] // KSPLIT

    def w_copy(s):
        at_s = pl.ds(pl.multiple_of(s * span, 256), span)
        return pltpu.make_async_copy(w_hbm.at[at_s], raw.at[at_s], wsem.at[s])

    for s in range(KSPLIT):
        w_copy(s).start()
    conv_cp = pltpu.make_async_copy(conv_hbm, convv, lsem.at[0])
    coef_cp = pltpu.make_async_copy(coef_hbm, coefv.at[pl.ds(0, wide)], lsem.at[1])
    step_cp = pltpu.make_async_copy(stepw_hbm, stepv, lsem.at[2])
    ssm_cp = pltpu.make_async_copy(ssm_hbm, ssmv, lsem.at[3])
    out_cp = pltpu.make_async_copy(outw_hbm, outv, lsem.at[4])
    for cp in (conv_cp, coef_cp, step_cp, ssm_cp, out_cp):
        cp.start()

    barrier = pltpu.get_barrier_semaphore()
    for k in range(1, n):
        pl.semaphore_signal(barrier, inc=1, device_id={"weight": (me + k) % n}, device_id_type=MESH)

    h = hidden[...].astype(F32)
    factor = lax.rsqrt(jnp.mean(h * h, axis=-1, keepdims=True) + 1e-05)
    nm = h * factor * gain[...]
    for c in range(ch):
        xs[pl.ds(c // cq * rows_dev * cq + c % cq, rows_dev, stride=cq), :] = nm[:, c * LANES : (c + 1) * LANES]
    for q in range(PARTS):
        xg[q, slot] = xs[pl.ds(q * rows_dev * cq, part), :].astype(BF16)
    coefv[pl.ds(wide, chunks * LANES - wide), :] = jnp.zeros((chunks * LANES - wide, chan), BF16)

    per = 256 // (2 * tiles)
    to, frm = iota((256, 256), 0), iota((256, 256), 1)
    branch, tile = to // per // tiles, to // per % tiles
    perm[...] = jnp.where(frm == to % per * (2 * tiles) + tile * 2 + branch, 1.0, 0.0).astype(BF16)
    group = min(GROUP, span // 256)

    def sort_weights(first, last):
        @pl.loop(first * (span // 256 // group), last * (span // 256 // group))
        def _(i):
            @pl.when(i % (span // 256 // group) == 0)
            def _():
                w_copy(i // (span // 256 // group)).wait()

            rhs = jnp.concatenate(
                [raw[pl.ds(pl.multiple_of((i * group + g) * 256, 256), 256), :] for g in range(group)], axis=1
            )
            e = dot(perm[...], rhs).astype(BF16)
            for g in range(group):
                at_g = pl.ds(pl.multiple_of((i * group + g) * per, 16), per)
                for b in range(2):
                    for j in range(tiles):
                        top = (b * tiles + j) * per
                        wd[b, at_g, j * LANES : (j + 1) * LANES] = e[top : top + per, g * LANES : (g + 1) * LANES]

    sort_weights(0, EARLY)
    pl.semaphore_wait(barrier, n - 1)

    sends = []

    def post(cp):
        cp.start()
        sends.append(cp)

    def slab_at(q, yy, cc):
        return xg.at[q, pl.ds(slab(yy, cc), outer)]

    for q in range(PARTS):
        for k in range(1, outer):
            post(rdma(xg.at[q, slot], xg.at[q, slot], a_s.at[q, k], a_r.at[q, k], at((z + k) % outer, y, core)))

    sort_weights(EARLY, KSPLIT)

    def widen(q, yy, cc):
        first = slab(yy, cc)
        xf[pl.ds(pl.multiple_of((q * n + first) * part, 16), outer * part), :] = (
            xg[q, pl.ds(first, outer)].reshape(outer * part, LANES).astype(F32)
        )

    for q in range(PARTS):
        for k in range(1, outer):
            src = xg.at[q, slab(y, core) + (z + outer - k) % outer]
            rdma(src, src, a_s.at[q, k], a_r.at[q, k], ypeer).wait_recv()
        src = slab_at(q, y, core)
        post(rdma(src, src, b_s.at[q], b_r.at[q], ypeer))
        post(rdma(src, src, c_s.at[q, 0], c_r.at[q, 0], cpeer))
        widen(q, y, core)
    for q in range(PARTS):
        src = slab_at(q, y, 1 - core)
        rdma(src, src, c_s.at[q, 0], c_r.at[q, 0], cpeer).wait_recv()
        widen(q, y, 1 - core)

    def take(q):
        src = slab_at(q, 1 - y, core)
        rdma(src, src, b_s.at[q], b_r.at[q], ypeer).wait_recv()
        post(rdma(src, src, c_s.at[q, 1], c_r.at[q, 1], cpeer))
        widen(q, 1 - y, core)

    total = jnp.zeros((rows, chan), F32)
    take(0)
    for q in range(PARTS):
        if q + 1 < PARTS:
            take(q + 1)
        src = slab_at(q, 1 - y, 1 - core)
        rdma(src, src, c_s.at[q, 1], c_r.at[q, 1], cpeer).wait_recv()
        widen(q, 1 - y, 1 - core)
        for c in range(cq):
            lhs[q, :, c * LANES : (c + 1) * LANES] = xf[
                pl.ds(q * n * part + c, rows, stride=cq), :
            ].astype(BF16)
        total = total + dot(lhs[q], wd[0, pl.ds(q * kpart, kpart), :])

    conv_cp.wait()
    ci = total.astype(BF16)
    r_at, c_at = iota((rows, allrows), 0), iota((rows, allrows), 1)
    pick = jnp.where(
        c_at == device_of(r_at // LIVE_MAX) * rows_dev + r_at % LIVE_MAX, 1.0, 0.0
    ).astype(BF16)
    total = ci.astype(F32) * convw[pl.ds(3, 1), :] + convo[...]
    for t in range(3):
        total = total + dot(pick, convv[t]) * convw[pl.ds(t, 1), :]
    x = (total / (1.0 + jnp.exp(-total))).astype(BF16)
    mx[...] = x.astype(F32)

    coef_cp.wait()
    low_part = lax.dot_general(x, coefv[...], (((1,), (1,)), ((), ())), preferred_element_type=F32)
    for c in range(chunks):
        lowf[pl.ds(c * rows, rows), :] = low_part[:, c * LANES : (c + 1) * LANES]
        lowp[pl.ds(c * rows, rows), :] = low_part[:, c * LANES : (c + 1) * LANES].astype(BF16)
    if n * lb > chunks * rows:
        spare = n * lb - chunks * rows
        lowf[pl.ds(chunks * rows, spare), :] = jnp.zeros((spare, LANES), F32)
        lowp[pl.ds(chunks * rows, spare), :] = jnp.zeros((spare, LANES), BF16)

    def low_at(ref, d):
        return ref.at[pl.ds(pl.multiple_of(d * lb, 16), lb)]

    for k in range(1, n):
        d = (me + k) % n
        post(rdma(low_at(lowp, d), lowr.at[k], d_s.at[k], d_r.at[k], d))

    g = jnp.zeros((rows, chan), F32)
    for q in range(PARTS):
        g = g + dot(lhs[q], wd[1, pl.ds(q * kpart, kpart), :])
    sgate[...] = g / (1.0 + jnp.exp(-g))
    erate[...] = jnp.exp(lograte[...])

    own = low_at(lowf, me)[...]
    for k in range(1, n):
        rdma(lowr.at[k], lowr.at[k], d_s.at[k], d_r.at[k], ypeer).wait_recv()
        own = own + lowr[k].astype(F32)
    low_at(lowg, me)[...] = own.astype(BF16)
    for k in range(1, n):
        d = (me + k) % n
        post(rdma(low_at(lowg, me), low_at(lowg, me), e_s.at[k], e_r.at[k], d))

    row4 = iota((allrows, chan), 0)
    count4 = jnp.zeros((allrows, chan), jnp.int32)
    for m in range(n):
        count4 = jnp.where(row4 // rows_dev == m, live[m], count4)
    alive4 = row4 % rows_dev < count4
    t_at, s_at = iota((allrows, rows), 1), iota((allrows, rows), 0)
    put = jnp.where(
        s_at == device_of(t_at // LIVE_MAX) * rows_dev + t_at % LIVE_MAX, 1.0, 0.0
    ).astype(BF16)
    for t in range(3):
        new = convv[t + 1].astype(F32) if t < 2 else dot(put, ci)
        newconv[t] = jnp.where(alive4, new, convv[t].astype(F32)).astype(BF16)
    conv_done = pltpu.make_async_copy(newconv, conv_out, osem.at[0])
    conv_done.start()
    step_cp.wait()
    ssm_cp.wait()

    for k in range(1, n):
        src = low_at(lowg, (me + n - k) % n)
        rdma(src, src, e_s.at[k], e_r.at[k], ypeer).wait_recv()

    low = jnp.concatenate([lowg[pl.ds(c * rows, rows), :] for c in range(DTR // LANES)], axis=1)
    v = dot(low, stepv[...]) + sbias[...]
    step[...] = jnp.maximum(v, 0.0) + jnp.log1p(jnp.exp(-jnp.abs(v)))
    coefs = lowg[pl.ds(DTR // LANES * rows, rows), :].astype(F32)
    for q in range(NSTATE):
        inb[pl.ds(q, rows, stride=NSTATE), :] = jnp.broadcast_to(coefs[:, q : q + 1], (rows, LANES))
        outb[pl.ds(q, rows, stride=NSTATE), :] = jnp.broadcast_to(
            coefs[:, NSTATE + q : NSTATE + q + 1], (rows, LANES)
        )

    @pl.loop(0, n)
    def _(m):
        count = live[m]
        for j in range(LIVE_MAX):
            r = slot_of(m) * LIVE_MAX + j
            old = ssmv[m * rows_dev + j].astype(F32)
            st = step[pl.ds(r, 1), :]
            xr = mx[pl.ds(r, 1), :]
            at_r = pl.ds(pl.multiple_of(r * NSTATE, NSTATE), NSTATE)
            inc = jnp.concatenate([inb[at_r, :]] * tiles, axis=1)
            outc = jnp.concatenate([outb[at_r, :]] * tiles, axis=1)
            upd = jnp.exp(-st * erate[...]) * old + st * inc * xr
            ro[pl.ds(r, 1), :] = jnp.sum(outc * upd, axis=0, keepdims=True)
            keep = jnp.full(old.shape, count, jnp.int32) > j
            ssmv[m * rows_dev + j] = jnp.where(keep, upd, old).astype(BF16)

    state_done = pltpu.make_async_copy(ssmv, state_out, osem.at[1])
    state_done.start()

    row3 = iota((rows, chan), 0)
    count3 = jnp.zeros((rows, chan), jnp.int32)
    for m in range(n):
        count3 = jnp.where(row3 // LIVE_MAX == slot_of(m), live[m], count3)
    read = (ro[...] + skip[...] * mx[...]) * sgate[...]
    gated = jnp.where(row3 % LIVE_MAX < count3, read, 0.0).astype(BF16)

    out_cp.wait()
    half = rows * cq // 2
    quarter = half // 2

    def project(u):
        p = dot(gated, outv[:, pl.ds(u * kpart, kpart)])
        for i in range(cq):
            pf[pl.ds(u * 2 * half + i, rows, stride=cq), :] = p[:, i * LANES : (i + 1) * LANES]
        s1[u] = pf[pl.ds(pl.multiple_of(u * 2 * half + (1 - core) * half, 16), half), :].astype(BF16)
        post(rdma(s1.at[u], r1.at[u], f_s.at[u], f_r.at[u], cpeer))

    def add_core(u):
        rdma(r1.at[u], r1.at[u], f_s.at[u], f_r.at[u], cpeer).wait_recv()
        far = pl.multiple_of((1 - y) * quarter, 16)
        near = pl.multiple_of(y * quarter, 16)
        base = pl.multiple_of(u * 2 * half + core * half, 16)
        s2[u] = (pf[pl.ds(base + far, quarter), :] + r1[u, pl.ds(far, quarter), :].astype(F32)).astype(BF16)
        post(rdma(s2.at[u], r2.at[u], g_s.at[u], g_r.at[u], ypeer))
        k1[u] = pf[pl.ds(base + near, quarter), :] + r1[u, pl.ds(near, quarter), :].astype(F32)

    def add_y(u):
        rdma(r2.at[u], r2.at[u], g_s.at[u], g_r.at[u], ypeer).wait_recv()
        both = k1[u] + r2[u].astype(F32)
        s3[u] = both.astype(BF16).reshape(outer, part, LANES)
        k2[u] = both.reshape(outer, part, LANES)
        for k in range(1, outer):
            zz = (z + k) % outer
            post(rdma(s3.at[u, zz], r3.at[u, k], h_s.at[u, k], h_r.at[u, k], at(zz, y, core)))

    fin[pl.ds(part, rows_dev * cq - part), :] = jnp.zeros((rows_dev * cq - part, LANES), F32)

    def finish(u):
        both = k2[u, z]
        for k in range(1, outer):
            rdma(r3.at[u, k], r3.at[u, k], h_s.at[u, k], h_r.at[u, k], ypeer).wait_recv()
            both = both + r3[u, k].astype(F32)
        fin[pl.ds(0, part), :] = both
        for c in range(cq):
            cols = slice((u * cq + c) * LANES, (u * cq + c + 1) * LANES)
            mixed[:, cols] = (hidden[:, cols].astype(F32) + fin[pl.ds(c, rows_dev, stride=cq), :]).astype(BF16)

    for u in range(PARTS):
        project(u)
        if u:
            add_core(u - 1)
    add_core(PARTS - 1)
    for u in range(PARTS):
        add_y(u)
    for u in range(PARTS):
        finish(u)
    for cp in sends:
        cp.wait_send()
    conv_done.wait()
    state_done.wait()


def hand_out(mixed, state, conv, mixed_out, state_out, conv_out, mixed_v, state_v, conv_v, sem_in, sem_out):
    half = state.shape[0] // 2
    trips = [
        (state.at[pl.ds(0, half)], state_v.at[pl.ds(0, half)], state_out.at[pl.ds(0, half)]),
        (state.at[pl.ds(half, half)], state_v.at[pl.ds(half, half)], state_out.at[pl.ds(half, half)]),
        (conv, conv_v, conv_out),
        (mixed, mixed_v, mixed_out),
    ]
    ins = [pltpu.make_async_copy(a, v, sem_in.at[i]) for i, (a, v, _) in enumerate(trips)]
    outs = [pltpu.make_async_copy(v, o, sem_out.at[i]) for i, (_, v, o) in enumerate(trips)]
    for cp in ins:
        cp.start()
    for first, second in zip(ins, outs):
        first.wait()
        second.start()
    for cp in outs:
        cp.wait()


def body(
    hidden, norm_gain, in_weight, conv_weight, conv_offset, coef_weight, step_weight,
    step_bias, log_rates, skip_gain, out_weight, ssm_state, conv_state, live_counts,
):
    n = lax.axis_size("weight")
    rows_dev, depth = hidden.shape
    chan = in_weight.shape[2]
    tiles = chan // LANES
    ch = depth // LANES
    rows = LIVE_MAX * n
    allrows = rows_dev * n
    outer = n // 4
    chunks = (DTR + 2 * NSTATE + LANES - 1) // LANES
    lb = -(-(chunks * rows) // (16 * n)) * 16
    cq = ch // PARTS
    part = LIVE_MAX * cq
    half = rows * cq // 2
    weight = in_weight.reshape(depth, 2, tiles, LANES).transpose(0, 2, 1, 3).reshape(depth * tiles * 2, LANES)
    vmem = pl.BlockSpec(memory_space=pltpu.VMEM)
    smem = pl.BlockSpec(memory_space=pltpu.SMEM)
    hbm = pl.BlockSpec(memory_space=pl.ANY)
    dma = pltpu.SemaphoreType.DMA
    V = pltpu.VMEM
    mixed, new_state, new_conv = pl.pallas_call(
        functools.partial(kernel, n, lb),
        out_shape=(
            jax.ShapeDtypeStruct(hidden.shape, BF16),
            jax.ShapeDtypeStruct(ssm_state.shape, BF16),
            jax.ShapeDtypeStruct((3, allrows, chan), BF16),
        ),
        in_specs=[vmem] * 7 + [smem] + [hbm] * 6,
        out_specs=(vmem, hbm, hbm),
        scratch_shapes=[
            V(weight.shape, BF16),
            V((256, 256), BF16),
            V((2, depth, chan), BF16),
            V((chunks * LANES, chan), BF16),
            V(step_weight.shape, BF16),
            V(out_weight.shape, BF16),
            V(ssm_state.shape, BF16),
            V((3, allrows, chan), BF16),
            V((3, allrows, chan), BF16),
            V((rows_dev * ch, LANES), F32),
            V((PARTS, n, part, LANES), BF16),
            V((PARTS * n * part, LANES), F32),
            V((PARTS, rows, depth // PARTS), BF16),
            V((rows, chan), F32),
            V((rows, chan), F32),
            V((rows, chan), F32),
            V((n * lb, LANES), BF16),
            V((n * lb, LANES), F32),
            V((n, lb, LANES), BF16),
            V((n * lb, LANES), BF16),
            V((rows * NSTATE, LANES), F32),
            V((rows * NSTATE, LANES), F32),
            V((rows, chan), F32),
            V((rows, chan), F32),
            V((NSTATE, chan), F32),
            V((PARTS * 2 * half, LANES), F32),
            V((PARTS, half, LANES), BF16),
            V((PARTS, half, LANES), BF16),
            V((PARTS, half // 2, LANES), F32),
            V((PARTS, half // 2, LANES), BF16),
            V((PARTS, half // 2, LANES), BF16),
            V((PARTS, outer, part, LANES), F32),
            V((PARTS, outer, part, LANES), BF16),
            V((PARTS, outer, part, LANES), BF16),
            V((rows_dev * cq, LANES), F32),
            dma((KSPLIT,)),
            dma((5,)),
            dma((2,)),
            dma((PARTS, outer)), dma((PARTS, outer)),
            dma((PARTS,)), dma((PARTS,)),
            dma((PARTS, 2)), dma((PARTS, 2)),
            dma((n,)), dma((n,)),
            dma((n,)), dma((n,)),
            dma((PARTS,)), dma((PARTS,)),
            dma((PARTS,)), dma((PARTS,)),
            dma((PARTS, outer)), dma((PARTS, outer)),
        ],
        compiler_params=pltpu.CompilerParams(
            collective_id=0, has_side_effects=True, vmem_limit_bytes=58 * 1024 * 1024
        ),
        name="mixer",
    )(
        hidden, norm_gain[None], conv_weight, conv_offset[None], step_bias[None], log_rates,
        skip_gain[None], live_counts,
        weight, coef_weight.T, step_weight, out_weight, ssm_state, conv_state.transpose(1, 0, 2),
    )
    mixed, new_state, new_conv = pl.pallas_call(
        hand_out,
        out_shape=tuple(jax.ShapeDtypeStruct(a.shape, a.dtype) for a in (mixed, new_state, new_conv)),
        in_specs=[hbm] * 3,
        out_specs=(hbm,) * 3,
        scratch_shapes=[V(a.shape, a.dtype) for a in (mixed, new_state, new_conv)] + [dma((4,)), dma((4,))],
        name="hand_out",
    )(mixed, new_state, new_conv)
    return mixed, new_state, new_conv.transpose(1, 0, 2)


def solution(mesh):
    in_specs = (
        P(("groups", "weight"), None),
        P(),
        P(None, None, "weight"),
        P(None, "weight"),
        P("weight"),
        P("weight", None),
        P(None, "weight"),
        P("weight"),
        P(None, "weight"),
        P("weight"),
        P("weight", None),
        P("groups", None, "weight"),
        P("groups", None, "weight"),
        P("groups"),
    )
    out_specs = (
        P(("groups", "weight"), None),
        P("groups", None, "weight"),
        P("groups", None, "weight"),
    )
    return jax.shard_map(body, mesh=mesh, in_specs=in_specs, out_specs=out_specs, check_vma=False)
```

```python
import functools

import jax
import jax.numpy as jnp
from jax import lax
from jax.experimental import pallas as pl
from jax.experimental.pallas import tpu as pltpu
from jax.sharding import PartitionSpec as P

NSTATE = 16
DTR = 512
LIVE_MAX = 3
LANES = 128
F32 = jnp.float32
BF16 = jnp.bfloat16
MESH = pl.DeviceIdType.MESH
KSPLIT = 8
PARTS = 4
SPREAD_IN = 2
SPREAD_OUT = 2
EARLY = 1
AHEAD = 0


def iota(shape, dim):
    return lax.broadcasted_iota(jnp.int32, shape, dim)


def dot(a, b):
    return jnp.dot(a, b, preferred_element_type=F32)


def kernel(
    n, lb,
    hidden_hbm, gain_hbm, convw_hbm, convo_hbm, sbias_hbm, lograte_hbm, skip_hbm, live_hbm,
    w_hbm, coef_hbm, stepw_hbm, outw_hbm, ssm_hbm, conv_hbm,
    mixed, newstate, newconv,
    hidden, gain, convw, convo, sbias, lograte, skip, live,
    raw, perm, wd, coefv, stepv, outv, ssmv, convv,
    xs, xg, xf, lhs, acc, mx, sgate, lowp, lowf, lowr, lowg, inb, outb, step, ro, erate,
    pf, s1, r1, k1, s2, r2, k2, s3, r3, fin,
    isem, wsem, lsem, osem, a_s, a_r, b_s, b_r, c_s, c_r, d_s, d_r, e_s, e_r, f_s, f_r, g_s, g_r, h_s, h_r,
):
    me = lax.axis_index("weight")
    core = me % 2
    y = (me // 2) % 2
    z = me // 4
    outer = n // 4
    depth = hidden.shape[1]
    rows_dev = hidden.shape[0]
    ch = depth // LANES
    cq = ch // PARTS
    part = LIVE_MAX * cq
    rows = LIVE_MAX * n
    allrows = rows_dev * n
    chan = wd.shape[2]
    tiles = chan // LANES
    kpart = depth // PARTS
    chunks = (DTR + 2 * NSTATE + LANES - 1) // LANES
    wide = DTR + 2 * NSTATE

    def at(zz, yy, cc):
        return zz * 4 + yy * 2 + cc

    def slab(yy, cc):
        return cc * (2 * outer) + yy * outer

    def device_of(s):
        return at(s % outer, (s // outer) % 2, s // (2 * outer))

    def slot_of(d):
        return slab((d // 2) % 2, d % 2) + d // 4

    ypeer = at(z, 1 - y, core)
    cpeer = at(z, y, 1 - core)
    slot = slab(y, core) + z

    def rdma(src, dst, send, recv, dev):
        return pltpu.make_async_remote_copy(
            src_ref=src, dst_ref=dst, send_sem=send, recv_sem=recv,
            device_id={"weight": dev}, device_id_type=MESH,
        )

    barrier = pltpu.get_barrier_semaphore()
    for k in range(1, n):
        pl.semaphore_signal(barrier, inc=1, device_id={"weight": (me + k) % n}, device_id_type=MESH)

    small = [
        pltpu.make_async_copy(src, dst, isem.at[i])
        for i, (src, dst) in enumerate((
            (hidden_hbm, hidden), (gain_hbm, gain), (convw_hbm, convw), (convo_hbm, convo),
            (sbias_hbm, sbias), (lograte_hbm, lograte), (skip_hbm, skip), (live_hbm, live),
        ))
    ]
    for cp in small:
        cp.start()
    span = raw.shape[0] // KSPLIT

    def w_copy(s):
        at_s = pl.ds(pl.multiple_of(s * span, 256), span)
        return pltpu.make_async_copy(w_hbm.at[at_s], raw.at[at_s], wsem.at[s])

    for s in range(KSPLIT):
        w_copy(s).start()
    conv_cp = pltpu.make_async_copy(conv_hbm, convv, lsem.at[0])
    coef_cp = pltpu.make_async_copy(coef_hbm, coefv.at[pl.ds(0, wide)], lsem.at[1])
    step_cp = pltpu.make_async_copy(stepw_hbm, stepv, lsem.at[2])
    ssm_cp = pltpu.make_async_copy(ssm_hbm, ssmv, lsem.at[3])
    out_cp = pltpu.make_async_copy(outw_hbm, outv, lsem.at[4])
    for cp in (conv_cp, coef_cp, step_cp, ssm_cp, out_cp):
        cp.start()

    small[0].wait()
    small[1].wait()
    h = hidden[...].astype(F32)
    factor = lax.rsqrt(jnp.mean(h * h, axis=-1, keepdims=True) + 1e-05)
    nm = h * factor * gain[...]
    for c in range(ch):
        xs[pl.ds(c // cq * rows_dev * cq + c % cq, rows_dev, stride=cq), :] = nm[:, c * LANES : (c + 1) * LANES]
    for q in range(PARTS):
        xg[q, slot] = xs[pl.ds(q * rows_dev * cq, part), :].astype(BF16)
    coefv[pl.ds(wide, chunks * LANES - wide), :] = jnp.zeros((chunks * LANES - wide, chan), BF16)

    per = 256 // (2 * tiles)
    to, frm = iota((128, 256), 0), iota((128, 256), 1)
    for b in range(2):
        perm[b] = jnp.where(frm == to % per * (2 * tiles) + to // per * 2 + b, 1.0, 0.0).astype(BF16)
    group = span // 256

    def sort_weights(b, first, last):
        @pl.loop(first, last)
        def _(i):
            if b == 0:
                w_copy(i).wait()
            rhs = jnp.concatenate(
                [raw[pl.ds(pl.multiple_of((i * group + g) * 256, 256), 256), :] for g in range(group)], axis=1
            )
            e = dot(perm[b], rhs).astype(BF16)
            for g in range(group):
                at_g = pl.ds(pl.multiple_of((i * group + g) * per, 16), per)
                for j in range(tiles):
                    wd[b, at_g, j * LANES : (j + 1) * LANES] = e[j * per : (j + 1) * per, g * LANES : (g + 1) * LANES]

    sort_weights(0, 0, EARLY)
    pl.semaphore_wait(barrier, n - 1)

    sends = []

    def post(cp):
        cp.start()
        sends.append(cp)

    def slab_at(q, yy, cc):
        return xg.at[q, pl.ds(slab(yy, cc), outer)]

    hops = [(flip, k) for flip in (1, 0) for k in range(outer) if flip or k]
    relayed = range(PARTS - SPREAD_IN)
    spread = range(PARTS - SPREAD_IN, PARTS)

    def there(flip, k):
        return at((z + k) % outer, (y + flip) % 2, core)

    for q in range(PARTS):
        for flip, k in hops:
            if q in spread or not flip:
                i = flip * outer + k
                post(rdma(xg.at[q, slot], xg.at[q, slot], a_s.at[q, i], a_r.at[q, i], there(flip, k)))

    sort_weights(0, EARLY, KSPLIT)
    sort_weights(1, 0, AHEAD)

    def widen(q, yy, cc):
        first = slab(yy, cc)
        xf[pl.ds(pl.multiple_of((q * n + first) * part, 16), outer * part), :] = (
            xg[q, pl.ds(first, outer)].reshape(outer * part, LANES).astype(F32)
        )

    def arrived(q, flip, k):
        i = flip * outer + k
        src = xg.at[q, slab((y + flip) % 2, core) + (z + outer - k) % outer]
        rdma(src, src, a_s.at[q, i], a_r.at[q, i], ypeer).wait_recv()

    def whole_at(q, cc):
        return xg.at[q, pl.ds(cc * (2 * outer), 2 * outer)]

    def multiply(q):
        for c in range(cq):
            lhs[q, :, c * LANES : (c + 1) * LANES] = xf[
                pl.ds(q * n * part + c, rows, stride=cq), :
            ].astype(BF16)
        return dot(lhs[q], wd[0, pl.ds(q * kpart, kpart), :])

    for q in relayed:
        for k in range(1, outer):
            arrived(q, 0, k)
        src = slab_at(q, y, core)
        post(rdma(src, src, b_s.at[q], b_r.at[q], ypeer))
        post(rdma(src, src, c_s.at[q, 0], c_r.at[q, 0], cpeer))
        widen(q, y, core)
    for q in spread:
        for flip, k in hops:
            arrived(q, flip, k)
        post(rdma(whole_at(q, core), whole_at(q, core), c_s.at[q, 0], c_r.at[q, 0], cpeer))
        widen(q, 0, core)
        widen(q, 1, core)
    for q in relayed:
        src = slab_at(q, y, 1 - core)
        rdma(src, src, c_s.at[q, 0], c_r.at[q, 0], cpeer).wait_recv()
        widen(q, y, 1 - core)

    total = jnp.zeros((rows, chan), F32)

    def relay(q):
        src = slab_at(q, 1 - y, core)
        rdma(src, src, b_s.at[q], b_r.at[q], ypeer).wait_recv()
        post(rdma(src, src, c_s.at[q, 1], c_r.at[q, 1], cpeer))
        widen(q, 1 - y, core)

    waiting = list(relayed)
    for q in spread:
        if waiting:
            relay(waiting.pop(0))
        rdma(whole_at(q, 1 - core), whole_at(q, 1 - core), c_s.at[q, 0], c_r.at[q, 0], cpeer).wait_recv()
        widen(q, 0, 1 - core)
        widen(q, 1, 1 - core)
        total = total + multiply(q)
    for q in relayed:
        if waiting:
            relay(waiting.pop(0))
        src = slab_at(q, 1 - y, 1 - core)
        rdma(src, src, c_s.at[q, 1], c_r.at[q, 1], cpeer).wait_recv()
        widen(q, 1 - y, 1 - core)
        total = total + multiply(q)

    for cp in small[2:]:
        cp.wait()
    conv_cp.wait()
    ci = total.astype(BF16)
    r_at, c_at = iota((rows, allrows), 0), iota((rows, allrows), 1)
    pick = jnp.where(
        c_at == device_of(r_at // LIVE_MAX) * rows_dev + r_at % LIVE_MAX, 1.0, 0.0
    ).astype(BF16)
    total = ci.astype(F32) * convw[pl.ds(3, 1), :] + convo[...]
    for t in range(3):
        total = total + dot(pick, convv[t]) * convw[pl.ds(t, 1), :]
    x = (total / (1.0 + jnp.exp(-total))).astype(BF16)
    mx[...] = x.astype(F32)

    coef_cp.wait()
    low_part = lax.dot_general(x, coefv[...], (((1,), (1,)), ((), ())), preferred_element_type=F32)
    for c in range(chunks):
        lowf[pl.ds(c * rows, rows), :] = low_part[:, c * LANES : (c + 1) * LANES]
        lowp[pl.ds(c * rows, rows), :] = low_part[:, c * LANES : (c + 1) * LANES].astype(BF16)
    if n * lb > chunks * rows:
        spare = n * lb - chunks * rows
        lowf[pl.ds(chunks * rows, spare), :] = jnp.zeros((spare, LANES), F32)
        lowp[pl.ds(chunks * rows, spare), :] = jnp.zeros((spare, LANES), BF16)

    def low_at(ref, d):
        return ref.at[pl.ds(pl.multiple_of(d * lb, 16), lb)]

    for k in range(1, n):
        d = (me + k) % n
        post(rdma(low_at(lowp, d), lowr.at[k], d_s.at[k], d_r.at[k], d))

    sort_weights(1, AHEAD, KSPLIT)

    own = low_at(lowf, me)[...]
    for k in range(1, n):
        rdma(lowr.at[k], lowr.at[k], d_s.at[k], d_r.at[k], ypeer).wait_recv()
        own = own + lowr[k].astype(F32)
    low_at(lowg, me)[...] = own.astype(BF16)
    for k in range(1, n):
        d = (me + k) % n
        post(rdma(low_at(lowg, me), low_at(lowg, me), e_s.at[k], e_r.at[k], d))

    g = jnp.zeros((rows, chan), F32)
    for q in range(PARTS):
        g = g + dot(lhs[q], wd[1, pl.ds(q * kpart, kpart), :])
    sgate[...] = g / (1.0 + jnp.exp(-g))
    erate[...] = jnp.exp(lograte[...])
    row4 = iota((allrows, chan), 0)
    count4 = jnp.zeros((allrows, chan), jnp.int32)
    for m in range(n):
        count4 = jnp.where(row4 // rows_dev == m, live[m], count4)
    alive4 = row4 % rows_dev < count4
    t_at, s_at = iota((allrows, rows), 1), iota((allrows, rows), 0)
    put = jnp.where(
        s_at == device_of(t_at // LIVE_MAX) * rows_dev + t_at % LIVE_MAX, 1.0, 0.0
    ).astype(BF16)
    for t in range(3):
        new = convv[t + 1].astype(F32) if t < 2 else dot(put, ci)
        newconv[t] = jnp.where(alive4, new, convv[t].astype(F32)).astype(BF16)
    step_cp.wait()
    ssm_cp.wait()

    for k in range(1, n):
        src = low_at(lowg, (me + n - k) % n)
        rdma(src, src, e_s.at[k], e_r.at[k], ypeer).wait_recv()

    low = jnp.concatenate([lowg[pl.ds(c * rows, rows), :] for c in range(DTR // LANES)], axis=1)
    v = dot(low, stepv[...]) + sbias[...]
    step[...] = jnp.maximum(v, 0.0) + jnp.log1p(jnp.exp(-jnp.abs(v)))
    coefs = lowg[pl.ds(DTR // LANES * rows, rows), :].astype(F32)
    for q in range(NSTATE):
        inb[pl.ds(q, rows, stride=NSTATE), :] = jnp.broadcast_to(coefs[:, q : q + 1], (rows, LANES))
        outb[pl.ds(q, rows, stride=NSTATE), :] = jnp.broadcast_to(
            coefs[:, NSTATE + q : NSTATE + q + 1], (rows, LANES)
        )

    @pl.loop(0, n, unroll=2)
    def _(m):
        count = live[m]
        newstate[m * rows_dev + LIVE_MAX] = ssmv[m * rows_dev + LIVE_MAX]
        for j in range(LIVE_MAX):
            r = slot_of(m) * LIVE_MAX + j
            old = ssmv[m * rows_dev + j].astype(F32)
            st = step[pl.ds(r, 1), :]
            xr = mx[pl.ds(r, 1), :]
            at_r = pl.ds(pl.multiple_of(r * NSTATE, NSTATE), NSTATE)
            inc = jnp.concatenate([inb[at_r, :]] * tiles, axis=1)
            outc = jnp.concatenate([outb[at_r, :]] * tiles, axis=1)
            upd = jnp.exp(-st * erate[...]) * old + st * inc * xr
            ro[pl.ds(r, 1), :] = jnp.sum(outc * upd, axis=0, keepdims=True)
            keep = jnp.full(old.shape, count, jnp.int32) > j
            newstate[m * rows_dev + j] = jnp.where(keep, upd, old).astype(BF16)


    row3 = iota((rows, chan), 0)
    count3 = jnp.zeros((rows, chan), jnp.int32)
    for m in range(n):
        count3 = jnp.where(row3 // LIVE_MAX == slot_of(m), live[m], count3)
    read = (ro[...] + skip[...] * mx[...]) * sgate[...]
    gated = jnp.where(row3 % LIVE_MAX < count3, read, 0.0).astype(BF16)

    out_cp.wait()
    half = rows * cq // 2
    quarter = half // 2

    def project(u):
        p = dot(gated, outv[:, pl.ds(u * kpart, kpart)])
        for i in range(cq):
            pf[pl.ds(u * 2 * half + i, rows, stride=cq), :] = p[:, i * LANES : (i + 1) * LANES]
        s1[u] = pf[pl.ds(pl.multiple_of(u * 2 * half + (1 - core) * half, 16), half), :].astype(BF16)
        post(rdma(s1.at[u], r1.at[u], f_s.at[u], f_r.at[u], cpeer))

    sent_by_y = range(PARTS - SPREAD_OUT)

    def add_core(u):
        rdma(r1.at[u], r1.at[u], f_s.at[u], f_r.at[u], cpeer).wait_recv()
        base = pl.multiple_of(u * 2 * half + core * half, 16)
        if u in sent_by_y:
            far = pl.multiple_of((1 - y) * quarter, 16)
            near = pl.multiple_of(y * quarter, 16)
            s2[u] = (pf[pl.ds(base + far, quarter), :] + r1[u, pl.ds(far, quarter), :].astype(F32)).astype(BF16)
            post(rdma(s2.at[u], r2.at[u], g_s.at[u], g_r.at[u], ypeer))
            k1[u] = pf[pl.ds(base + near, quarter), :] + r1[u, pl.ds(near, quarter), :].astype(F32)
        else:
            both = pf[pl.ds(base, half), :] + r1[u].astype(F32)
            s3[u] = both.astype(BF16).reshape(2 * outer, part, LANES)
            k2[u] = both.reshape(2 * outer, part, LANES)
            for flip, k in hops:
                i = flip * outer + k
                block = (y + flip) % 2 * outer + (z + k) % outer
                post(rdma(s3.at[u, block], r3.at[u, i], h_s.at[u, i], h_r.at[u, i], there(flip, k)))

    def add_y(u):
        rdma(r2.at[u], r2.at[u], g_s.at[u], g_r.at[u], ypeer).wait_recv()
        both = k1[u] + r2[u].astype(F32)
        s3[u, pl.ds(0, outer)] = both.astype(BF16).reshape(outer, part, LANES)
        k2[u, pl.ds(0, outer)] = both.reshape(outer, part, LANES)
        for k in range(1, outer):
            post(rdma(s3.at[u, (z + k) % outer], r3.at[u, k], h_s.at[u, k], h_r.at[u, k], there(0, k)))

    fin[pl.ds(part, rows_dev * cq - part), :] = jnp.zeros((rows_dev * cq - part, LANES), F32)

    def finish(u):
        both = k2[u, z if u in sent_by_y else y * outer + z]
        for flip, k in hops:
            if u in sent_by_y and flip:
                continue
            i = flip * outer + k
            rdma(r3.at[u, i], r3.at[u, i], h_s.at[u, i], h_r.at[u, i], ypeer).wait_recv()
            both = both + r3[u, i].astype(F32)
        fin[pl.ds(0, part), :] = both
        for c in range(cq):
            cols = slice((u * cq + c) * LANES, (u * cq + c + 1) * LANES)
            mixed[:, cols] = (hidden[:, cols].astype(F32) + fin[pl.ds(c, rows_dev, stride=cq), :]).astype(BF16)

    for u in range(PARTS):
        project(u)
        if u:
            add_core(u - 1)
    add_core(PARTS - 1)
    for u in sent_by_y:
        add_y(u)
    for u in [u for u in range(PARTS) if u not in sent_by_y] + list(sent_by_y):
        finish(u)
    for cp in sends:
        cp.wait_send()


def hand_out(mixed, state, conv, mixed_out, state_out, conv_out, sem):
    step = state.shape[0] // 4
    trips = [(state.at[pl.ds(i * step, step)], state_out.at[pl.ds(i * step, step)]) for i in range(4)]
    trips += [(conv, conv_out), (mixed, mixed_out)]
    copies = [pltpu.make_async_copy(a, o, sem.at[i]) for i, (a, o) in enumerate(trips)]
    for cp in copies:
        cp.start()
    for cp in copies:
        cp.wait()


def body(
    hidden, norm_gain, in_weight, conv_weight, conv_offset, coef_weight, step_weight,
    step_bias, log_rates, skip_gain, out_weight, ssm_state, conv_state, live_counts,
):
    n = lax.axis_size("weight")
    rows_dev, depth = hidden.shape
    chan = in_weight.shape[2]
    tiles = chan // LANES
    ch = depth // LANES
    rows = LIVE_MAX * n
    allrows = rows_dev * n
    outer = n // 4
    chunks = (DTR + 2 * NSTATE + LANES - 1) // LANES
    lb = -(-(chunks * rows) // (16 * n)) * 16
    cq = ch // PARTS
    part = LIVE_MAX * cq
    half = rows * cq // 2
    weight = in_weight.reshape(depth, 2, tiles, LANES).transpose(0, 2, 1, 3).reshape(depth * tiles * 2, LANES)
    vmem = pl.BlockSpec(memory_space=pltpu.VMEM)
    hbm = pl.BlockSpec(memory_space=pl.ANY)
    dma = pltpu.SemaphoreType.DMA
    V = pltpu.VMEM
    mixed, new_state, new_conv = pl.pallas_call(
        functools.partial(kernel, n, lb),
        out_shape=(
            V(hidden.shape, BF16),
            V(ssm_state.shape, BF16),
            V((3, allrows, chan), BF16),
        ),
        in_specs=[hbm] * 14,
        out_specs=(vmem,) * 3,
        scratch_shapes=[
            V(hidden.shape, BF16),
            V((1, depth), F32),
            V(conv_weight.shape, F32),
            V((1, chan), F32),
            V((1, chan), F32),
            V(log_rates.shape, F32),
            V((1, chan), F32),
            pltpu.SMEM(live_counts.shape, jnp.int32),
            V(weight.shape, BF16),
            V((2, 128, 256), BF16),
            V((2, depth, chan), BF16),
            V((chunks * LANES, chan), BF16),
            V(step_weight.shape, BF16),
            V(out_weight.shape, BF16),
            V(ssm_state.shape, BF16),
            V((3, allrows, chan), BF16),
            V((rows_dev * ch, LANES), F32),
            V((PARTS, n, part, LANES), BF16),
            V((PARTS * n * part, LANES), F32),
            V((PARTS, rows, depth // PARTS), BF16),
            V((rows, chan), F32),
            V((rows, chan), F32),
            V((rows, chan), F32),
            V((n * lb, LANES), BF16),
            V((n * lb, LANES), F32),
            V((n, lb, LANES), BF16),
            V((n * lb, LANES), BF16),
            V((rows * NSTATE, LANES), F32),
            V((rows * NSTATE, LANES), F32),
            V((rows, chan), F32),
            V((rows, chan), F32),
            V((NSTATE, chan), F32),
            V((PARTS * 2 * half, LANES), F32),
            V((PARTS, half, LANES), BF16),
            V((PARTS, half, LANES), BF16),
            V((PARTS, half // 2, LANES), F32),
            V((PARTS, half // 2, LANES), BF16),
            V((PARTS, half // 2, LANES), BF16),
            V((PARTS, 2 * outer, part, LANES), F32),
            V((PARTS, 2 * outer, part, LANES), BF16),
            V((PARTS, 2 * outer, part, LANES), BF16),
            V((rows_dev * cq, LANES), F32),
            dma((8,)),
            dma((KSPLIT,)),
            dma((5,)),
            dma((2,)),
            dma((PARTS, 2 * outer)), dma((PARTS, 2 * outer)),
            dma((PARTS,)), dma((PARTS,)),
            dma((PARTS, 2)), dma((PARTS, 2)),
            dma((n,)), dma((n,)),
            dma((n,)), dma((n,)),
            dma((PARTS,)), dma((PARTS,)),
            dma((PARTS,)), dma((PARTS,)),
            dma((PARTS, 2 * outer)), dma((PARTS, 2 * outer)),
        ],
        compiler_params=pltpu.CompilerParams(
            collective_id=0, has_side_effects=True, vmem_limit_bytes=58 * 1024 * 1024
        ),
        name="mixer",
    )(
        hidden, norm_gain[None], conv_weight, conv_offset[None], step_bias[None], log_rates,
        skip_gain[None], live_counts,
        weight, coef_weight.T, step_weight, out_weight, ssm_state, conv_state.transpose(1, 0, 2),
    )
    mixed, new_state, new_conv = pl.pallas_call(
        hand_out,
        out_shape=tuple(jax.ShapeDtypeStruct(a.shape, a.dtype) for a in (mixed, new_state, new_conv)),
        in_specs=[vmem] * 3,
        out_specs=(hbm,) * 3,
        scratch_shapes=[dma((6,))],
        name="hand_out",
    )(*(pltpu.with_memory_space_constraint(v, pltpu.VMEM) for v in (mixed, new_state, new_conv)))
    return mixed, new_state, new_conv.transpose(1, 0, 2)


def solution(mesh):
    in_specs = (
        P(("groups", "weight"), None),
        P(),
        P(None, None, "weight"),
        P(None, "weight"),
        P("weight"),
        P("weight", None),
        P(None, "weight"),
        P("weight"),
        P(None, "weight"),
        P("weight"),
        P("weight", None),
        P("groups", None, "weight"),
        P("groups", None, "weight"),
        P("groups"),
    )
    out_specs = (
        P(("groups", "weight"), None),
        P("groups", None, "weight"),
        P("groups", None, "weight"),
    )
    return jax.shard_map(body, mesh=mesh, in_specs=in_specs, out_specs=out_specs, check_vma=False)
```

```python
import functools

import jax
import jax.numpy as jnp
from jax import lax
from jax.experimental import pallas as pl
from jax.experimental.pallas import tpu as pltpu
from jax.sharding import PartitionSpec as P

NSTATE = 16
DTR = 512
LIVE_MAX = 3
LANES = 128
F32 = jnp.float32
BF16 = jnp.bfloat16
MESH = pl.DeviceIdType.MESH
KSPLIT = 8
PARTS = 4
LOG2E = 1.4426950408889634
SPREAD_IN = 2
SPREAD_OUT = 2
EARLY = 1
AHEAD = 0


def iota(shape, dim):
    return lax.broadcasted_iota(jnp.int32, shape, dim)


def dot(a, b):
    return jnp.dot(a, b, preferred_element_type=F32)


def kernel(
    n, lb,
    hidden_hbm, gain_hbm, convw_hbm, convo_hbm, sbias_hbm, lograte_hbm, skip_hbm, live_hbm,
    w_hbm, coef_hbm, stepw_hbm, outw_hbm, ssm_hbm, conv_hbm,
    mixed, newstate, newconv,
    hidden, gain, convw, convo, sbias, lograte, skip, live,
    raw, perm, wd, coefv, stepv, outv, ssmv, convv,
    xs, xg, xf, lhs, acc, mx, sgate, lowp, lowf, lowr, lowg, inb, outb, step, push, ro, erate,
    pf, mine, s1, r1, k1, s2, r2, k2, s3, r3, fin,
    isem, wsem, lsem, osem, a_s, a_r, b_s, b_r, c_s, c_r, d_s, d_r, e_s, e_r, f_s, f_r, g_s, g_r, h_s, h_r,
):
    me = lax.axis_index("weight")
    core = me % 2
    y = (me // 2) % 2
    z = me // 4
    outer = n // 4
    depth = hidden.shape[1]
    rows_dev = hidden.shape[0]
    ch = depth // LANES
    cq = ch // PARTS
    part = LIVE_MAX * cq
    rows = LIVE_MAX * n
    allrows = rows_dev * n
    chan = wd.shape[2]
    tiles = chan // LANES
    kpart = depth // PARTS
    chunks = (DTR + 2 * NSTATE + LANES - 1) // LANES
    wide = DTR + 2 * NSTATE

    def at(zz, yy, cc):
        return zz * 4 + yy * 2 + cc

    def slab(yy, cc):
        return cc * (2 * outer) + yy * outer

    def device_of(s):
        return at(s % outer, (s // outer) % 2, s // (2 * outer))

    def slot_of(d):
        return slab((d // 2) % 2, d % 2) + d // 4

    ypeer = at(z, 1 - y, core)
    cpeer = at(z, y, 1 - core)
    slot = slab(y, core) + z

    def rdma(src, dst, send, recv, dev):
        return pltpu.make_async_remote_copy(
            src_ref=src, dst_ref=dst, send_sem=send, recv_sem=recv,
            device_id={"weight": dev}, device_id_type=MESH,
        )

    barrier = pltpu.get_barrier_semaphore()
    for k in range(1, n):
        pl.semaphore_signal(barrier, inc=1, device_id={"weight": (me + k) % n}, device_id_type=MESH)

    small = [
        pltpu.make_async_copy(src, dst, isem.at[i])
        for i, (src, dst) in enumerate((
            (hidden_hbm, hidden), (gain_hbm, gain), (convw_hbm, convw), (convo_hbm, convo),
            (sbias_hbm, sbias), (lograte_hbm, lograte), (skip_hbm, skip), (live_hbm, live),
        ))
    ]
    for cp in small:
        cp.start()
    span = raw.shape[0] // KSPLIT

    def w_copy(s):
        at_s = pl.ds(pl.multiple_of(s * span, 256), span)
        return pltpu.make_async_copy(w_hbm.at[at_s], raw.at[at_s], wsem.at[s])

    for s in range(KSPLIT):
        w_copy(s).start()
    conv_cp = pltpu.make_async_copy(conv_hbm, convv, lsem.at[0])
    coef_cp = pltpu.make_async_copy(coef_hbm, coefv.at[pl.ds(0, wide)], lsem.at[1])
    step_cp = pltpu.make_async_copy(stepw_hbm, stepv, lsem.at[2])
    ssm_cp = pltpu.make_async_copy(ssm_hbm, ssmv, lsem.at[3])
    out_cp = pltpu.make_async_copy(outw_hbm, outv, lsem.at[4])
    for cp in (conv_cp, coef_cp, step_cp, ssm_cp, out_cp):
        cp.start()

    small[0].wait()
    small[1].wait()
    h = hidden[...].astype(F32)
    factor = lax.rsqrt(jnp.mean(h * h, axis=-1, keepdims=True) + 1e-05)
    nm = h * factor * gain[...]
    for c in range(ch):
        xs[pl.ds(c // cq * rows_dev * cq + c % cq, rows_dev, stride=cq), :] = nm[:, c * LANES : (c + 1) * LANES]
    for q in range(PARTS):
        xg[q, slot] = xs[pl.ds(q * rows_dev * cq, part), :].astype(BF16)
    coefv[pl.ds(wide, chunks * LANES - wide), :] = jnp.zeros((chunks * LANES - wide, chan), BF16)

    per = 256 // (2 * tiles)
    to, frm = iota((128, 256), 0), iota((128, 256), 1)
    for b in range(2):
        perm[b] = jnp.where(frm == to % per * (2 * tiles) + to // per * 2 + b, 1.0, 0.0).astype(BF16)
    group = span // 256

    def sort_weights(b, first, last):
        @pl.loop(first, last)
        def _(i):
            if b == 0:
                w_copy(i).wait()
            rhs = jnp.concatenate(
                [raw[pl.ds(pl.multiple_of((i * group + g) * 256, 256), 256), :] for g in range(group)], axis=1
            )
            e = dot(perm[b], rhs).astype(BF16)
            for g in range(group):
                at_g = pl.ds(pl.multiple_of((i * group + g) * per, 16), per)
                for j in range(tiles):
                    wd[b, at_g, j * LANES : (j + 1) * LANES] = e[j * per : (j + 1) * per, g * LANES : (g + 1) * LANES]

    sort_weights(0, 0, EARLY)
    pl.semaphore_wait(barrier, n - 1)

    sends = []

    def post(cp):
        cp.start()
        sends.append(cp)

    def settle(count):
        for cp in sends[:count]:
            cp.wait_send()
        del sends[:count]

    def slab_at(q, yy, cc):
        return xg.at[q, pl.ds(slab(yy, cc), outer)]

    hops = [(flip, k) for flip in (1, 0) for k in range(outer) if flip or k]
    relayed = range(PARTS - SPREAD_IN)
    spread = range(PARTS - SPREAD_IN, PARTS)

    def there(flip, k):
        return at((z + k) % outer, (y + flip) % 2, core)

    for q in range(PARTS):
        for flip, k in hops:
            if q in spread or not flip:
                i = flip * outer + k
                post(rdma(xg.at[q, slot], xg.at[q, slot], a_s.at[q, i], a_r.at[q, i], there(flip, k)))

    sort_weights(0, EARLY, KSPLIT)
    sort_weights(1, 0, AHEAD)

    def widen(q, yy, cc):
        first = slab(yy, cc)
        xf[pl.ds(pl.multiple_of((q * n + first) * part, 16), outer * part), :] = (
            xg[q, pl.ds(first, outer)].reshape(outer * part, LANES).astype(F32)
        )

    def arrived(q, flip, k):
        i = flip * outer + k
        src = xg.at[q, slab((y + flip) % 2, core) + (z + outer - k) % outer]
        rdma(src, src, a_s.at[q, i], a_r.at[q, i], ypeer).wait_recv()

    def whole_at(q, cc):
        return xg.at[q, pl.ds(cc * (2 * outer), 2 * outer)]

    def multiply(q):
        for c in range(cq):
            lhs[q, :, c * LANES : (c + 1) * LANES] = xf[
                pl.ds(q * n * part + c, rows, stride=cq), :
            ].astype(BF16)
        return dot(lhs[q], wd[0, pl.ds(q * kpart, kpart), :])

    for q in relayed:
        for k in range(1, outer):
            arrived(q, 0, k)
        src = slab_at(q, y, core)
        post(rdma(src, src, b_s.at[q], b_r.at[q], ypeer))
        post(rdma(src, src, c_s.at[q, 0], c_r.at[q, 0], cpeer))
        widen(q, y, core)
    for q in spread:
        for flip, k in hops:
            arrived(q, flip, k)
        post(rdma(whole_at(q, core), whole_at(q, core), c_s.at[q, 0], c_r.at[q, 0], cpeer))
        widen(q, 0, core)
        widen(q, 1, core)
    for q in relayed:
        src = slab_at(q, y, 1 - core)
        rdma(src, src, c_s.at[q, 0], c_r.at[q, 0], cpeer).wait_recv()
        widen(q, y, 1 - core)

    total = jnp.zeros((rows, chan), F32)

    def relay(q):
        src = slab_at(q, 1 - y, core)
        rdma(src, src, b_s.at[q], b_r.at[q], ypeer).wait_recv()
        post(rdma(src, src, c_s.at[q, 1], c_r.at[q, 1], cpeer))
        widen(q, 1 - y, core)

    waiting = list(relayed)
    for q in spread:
        if waiting:
            relay(waiting.pop(0))
        rdma(whole_at(q, 1 - core), whole_at(q, 1 - core), c_s.at[q, 0], c_r.at[q, 0], cpeer).wait_recv()
        widen(q, 0, 1 - core)
        widen(q, 1, 1 - core)
        total = total + multiply(q)
    for q in relayed:
        if waiting:
            relay(waiting.pop(0))
        src = slab_at(q, 1 - y, 1 - core)
        rdma(src, src, c_s.at[q, 1], c_r.at[q, 1], cpeer).wait_recv()
        widen(q, 1 - y, 1 - core)
        total = total + multiply(q)

    for cp in small[2:]:
        cp.wait()
    conv_cp.wait()
    ci = total.astype(BF16)
    r_at, c_at = iota((rows, allrows), 0), iota((rows, allrows), 1)
    pick = jnp.where(
        c_at == device_of(r_at // LIVE_MAX) * rows_dev + r_at % LIVE_MAX, 1.0, 0.0
    ).astype(BF16)
    total = ci.astype(F32) * convw[pl.ds(3, 1), :] + convo[...]
    for t in range(3):
        total = total + dot(pick, convv[t]) * convw[pl.ds(t, 1), :]
    x = (total / (1.0 + jnp.exp(-total))).astype(BF16)
    mx[...] = x.astype(F32)

    coef_cp.wait()
    low_part = lax.dot_general(x, coefv[...], (((1,), (1,)), ((), ())), preferred_element_type=F32)
    for c in range(chunks):
        lowf[pl.ds(c * rows, rows), :] = low_part[:, c * LANES : (c + 1) * LANES]
        lowp[pl.ds(c * rows, rows), :] = low_part[:, c * LANES : (c + 1) * LANES].astype(BF16)
    if lowp.shape[0] > chunks * rows:
        spare = lowp.shape[0] - chunks * rows
        lowf[pl.ds(chunks * rows, spare), :] = jnp.zeros((spare, LANES), F32)
        lowp[pl.ds(chunks * rows, spare), :] = jnp.zeros((spare, LANES), BF16)

    gathered = len(sends)

    def low_at(ref, d):
        return ref.at[pl.ds(pl.multiple_of(d * lb, 16), lb)]

    count = n // 2
    first_owner = outer // 4 * 4
    mine_low = (me + n - first_owner) % n
    owner = mine_low < count

    def to_owner(k):
        d = first_owner + (me + k) % count
        return rdma(low_at(lowp, d - first_owner), lowr.at[me], d_s.at[k], d_r.at[me], d), d != me

    for k in range(count):
        cp, other = to_owner(k)
        pl.when(other)(cp.start)

    settle(gathered)
    sort_weights(1, AHEAD, KSPLIT)

    def from_owner(k):
        src = low_at(lowg, mine_low % count)
        return rdma(src, src, e_s.at[k], e_r.at[mine_low % count], (me + k) % n)

    @pl.when(owner)
    def _():
        own = low_at(lowf, mine_low % count)[...]
        for k in range(1, n):
            sender = (me + k) % n
            rdma(lowr.at[sender], lowr.at[sender], d_s.at[0], d_r.at[sender], ypeer).wait_recv()
            own = own + lowr[sender].astype(F32)
        low_at(lowg, mine_low % count)[...] = own.astype(BF16)
        for k in range(1, n):
            from_owner(k).start()

    g = jnp.zeros((rows, chan), F32)
    for q in range(PARTS):
        g = g + dot(lhs[q], wd[1, pl.ds(q * kpart, kpart), :])
    sgate[...] = g / (1.0 + jnp.exp(-g))
    erate[...] = jnp.exp(lograte[...]) * (-LOG2E)
    for k in range(count):
        cp, other = to_owner(k)
        pl.when(other)(cp.wait_send)
    row4 = iota((allrows, chan), 0)
    count4 = jnp.zeros((allrows, chan), jnp.int32)
    for m in range(n):
        count4 = jnp.where(row4 // rows_dev == m, live[m], count4)
    alive4 = row4 % rows_dev < count4
    t_at, s_at = iota((allrows, rows), 1), iota((allrows, rows), 0)
    put = jnp.where(
        s_at == device_of(t_at // LIVE_MAX) * rows_dev + t_at % LIVE_MAX, 1.0, 0.0
    ).astype(BF16)
    for t in range(3):
        new = convv[t + 1].astype(F32) if t < 2 else dot(put, ci)
        newconv[t] = jnp.where(alive4, new, convv[t].astype(F32)).astype(BF16)
    step_cp.wait()
    ssm_cp.wait()

    for o in range(count):
        src = low_at(lowg, o)
        cp = rdma(src, src, e_s.at[0], e_r.at[o], ypeer)
        pl.when(first_owner + o != me)(cp.wait_recv)

    low = jnp.concatenate([lowg[pl.ds(c * rows, rows), :] for c in range(DTR // LANES)], axis=1)
    v = dot(low, stepv[...]) + sbias[...]
    step[...] = jnp.maximum(v, 0.0) + jnp.log1p(jnp.exp(-jnp.abs(v)))
    push[...] = step[...] * mx[...]
    coefs = lowg[pl.ds(DTR // LANES * rows, rows), :].astype(F32)
    for q in range(NSTATE):
        inb[pl.ds(q, rows, stride=NSTATE), :] = jnp.broadcast_to(coefs[:, q : q + 1], (rows, LANES))
        outb[pl.ds(q, rows, stride=NSTATE), :] = jnp.broadcast_to(
            coefs[:, NSTATE + q : NSTATE + q + 1], (rows, LANES)
        )

    @pl.loop(0, n, unroll=2)
    def _(m):
        alive = live[m]
        newstate[m * rows_dev + LIVE_MAX] = ssmv[m * rows_dev + LIVE_MAX]
        for j in range(LIVE_MAX):
            r = slot_of(m) * LIVE_MAX + j
            old = ssmv[m * rows_dev + j].astype(F32)
            st = step[pl.ds(r, 1), :]
            sx = push[pl.ds(r, 1), :]
            at_r = pl.ds(pl.multiple_of(r * NSTATE, NSTATE), NSTATE)
            inc = jnp.concatenate([inb[at_r, :]] * tiles, axis=1)
            outc = jnp.concatenate([outb[at_r, :]] * tiles, axis=1)
            upd = jnp.exp2(st * erate[...]) * old + inc * sx
            ro[pl.ds(r, 1), :] = jnp.sum(outc * upd, axis=0, keepdims=True)
            keep = jnp.full(old.shape, alive, jnp.int32) > j
            newstate[m * rows_dev + j] = jnp.where(keep, upd, old).astype(BF16)


    row3 = iota((rows, chan), 0)
    count3 = jnp.zeros((rows, chan), jnp.int32)
    for m in range(n):
        count3 = jnp.where(row3 // LIVE_MAX == slot_of(m), live[m], count3)
    read = (ro[...] + skip[...] * mx[...]) * sgate[...]
    gated = jnp.where(row3 % LIVE_MAX < count3, read, 0.0).astype(BF16)

    out_cp.wait()
    half = rows * cq // 2
    quarter = half // 2

    def project(u):
        p = dot(gated, outv[:, pl.ds(u * kpart, kpart)])
        low_half, high_half = p[: rows // 2], p[rows // 2 :]
        first = jnp.full(low_half.shape, core, jnp.int32) == 0
        s1[u] = jnp.where(first, high_half, low_half).astype(BF16)
        post(rdma(s1.at[u], r1.at[u], f_s.at[u], f_r.at[u], cpeer))
        mine[u] = jnp.where(first, low_half, high_half)

    sent_by_y = range(PARTS - SPREAD_OUT)

    def add_core(u):
        rdma(r1.at[u], r1.at[u], f_s.at[u], f_r.at[u], cpeer).wait_recv()
        base = u * half
        both = mine[u] + r1[u].astype(F32)
        for i in range(cq):
            pf[pl.ds(base + i, rows // 2, stride=cq), :] = both[:, i * LANES : (i + 1) * LANES]
        if u in sent_by_y:
            far = pl.multiple_of((1 - y) * quarter, 16)
            near = pl.multiple_of(y * quarter, 16)
            s2[u] = pf[pl.ds(base + far, quarter), :].astype(BF16)
            post(rdma(s2.at[u], r2.at[u], g_s.at[u], g_r.at[u], ypeer))
            k1[u] = pf[pl.ds(base + near, quarter), :]
        else:
            both = pf[pl.ds(base, half), :]
            s3[u] = both.astype(BF16).reshape(2 * outer, part, LANES)
            k2[u] = both.reshape(2 * outer, part, LANES)
            for flip, k in hops:
                i = flip * outer + k
                block = (y + flip) % 2 * outer + (z + k) % outer
                post(rdma(s3.at[u, block], r3.at[u, i], h_s.at[u, i], h_r.at[u, i], there(flip, k)))

    def add_y(u):
        rdma(r2.at[u], r2.at[u], g_s.at[u], g_r.at[u], ypeer).wait_recv()
        both = k1[u] + r2[u].astype(F32)
        s3[u, pl.ds(0, outer)] = both.astype(BF16).reshape(outer, part, LANES)
        k2[u, pl.ds(0, outer)] = both.reshape(outer, part, LANES)
        for k in range(1, outer):
            post(rdma(s3.at[u, (z + k) % outer], r3.at[u, k], h_s.at[u, k], h_r.at[u, k], there(0, k)))

    fin[pl.ds(part, rows_dev * cq - part), :] = jnp.zeros((rows_dev * cq - part, LANES), F32)

    def finish(u):
        both = k2[u, z if u in sent_by_y else y * outer + z]
        for flip, k in hops:
            if u in sent_by_y and flip:
                continue
            i = flip * outer + k
            rdma(r3.at[u, i], r3.at[u, i], h_s.at[u, i], h_r.at[u, i], ypeer).wait_recv()
            both = both + r3[u, i].astype(F32)
        fin[pl.ds(0, part), :] = both
        for c in range(cq):
            cols = slice((u * cq + c) * LANES, (u * cq + c + 1) * LANES)
            mixed[:, cols] = (hidden[:, cols].astype(F32) + fin[pl.ds(c, rows_dev, stride=cq), :]).astype(BF16)

    summed = len(sends)
    for u in range(PARTS):
        project(u)
        if u:
            add_core(u - 1)
    add_core(PARTS - 1)
    settle(summed)

    @pl.when(owner)
    def _():
        for k in range(1, n):
            from_owner(k).wait_send()

    for u in sent_by_y:
        add_y(u)
    settle(len(sends) - (outer - 1))
    for u in [u for u in range(PARTS) if u not in sent_by_y] + list(sent_by_y):
        finish(u)
    for cp in sends:
        cp.wait_send()


def hand_out(mixed, state, conv, mixed_out, state_out, conv_out, sem):
    step = state.shape[0] // 4
    trips = [(state.at[pl.ds(i * step, step)], state_out.at[pl.ds(i * step, step)]) for i in range(4)]
    trips += [(conv, conv_out), (mixed, mixed_out)]
    copies = [pltpu.make_async_copy(a, o, sem.at[i]) for i, (a, o) in enumerate(trips)]
    for cp in copies:
        cp.start()
    for cp in copies:
        cp.wait()


def body(
    hidden, norm_gain, in_weight, conv_weight, conv_offset, coef_weight, step_weight,
    step_bias, log_rates, skip_gain, out_weight, ssm_state, conv_state, live_counts,
):
    n = lax.axis_size("weight")
    rows_dev, depth = hidden.shape
    chan = in_weight.shape[2]
    tiles = chan // LANES
    ch = depth // LANES
    rows = LIVE_MAX * n
    allrows = rows_dev * n
    outer = n // 4
    chunks = (DTR + 2 * NSTATE + LANES - 1) // LANES
    lb = -(-(chunks * rows) // (8 * n)) * 16
    cq = ch // PARTS
    part = LIVE_MAX * cq
    half = rows * cq // 2
    weight = in_weight.reshape(depth, 2, tiles, LANES).transpose(0, 2, 1, 3).reshape(depth * tiles * 2, LANES)
    vmem = pl.BlockSpec(memory_space=pltpu.VMEM)
    hbm = pl.BlockSpec(memory_space=pl.ANY)
    dma = pltpu.SemaphoreType.DMA
    V = pltpu.VMEM
    mixed, new_state, new_conv = pl.pallas_call(
        functools.partial(kernel, n, lb),
        out_shape=(
            V(hidden.shape, BF16),
            V(ssm_state.shape, BF16),
            V((3, allrows, chan), BF16),
        ),
        in_specs=[hbm] * 14,
        out_specs=(vmem,) * 3,
        scratch_shapes=[
            V(hidden.shape, BF16),
            V((1, depth), F32),
            V(conv_weight.shape, F32),
            V((1, chan), F32),
            V((1, chan), F32),
            V(log_rates.shape, F32),
            V((1, chan), F32),
            pltpu.SMEM(live_counts.shape, jnp.int32),
            V(weight.shape, BF16),
            V((2, 128, 256), BF16),
            V((2, depth, chan), BF16),
            V((chunks * LANES, chan), BF16),
            V(step_weight.shape, BF16),
            V(out_weight.shape, BF16),
            V(ssm_state.shape, BF16),
            V((3, allrows, chan), BF16),
            V((rows_dev * ch, LANES), F32),
            V((PARTS, n, part, LANES), BF16),
            V((PARTS * n * part, LANES), F32),
            V((PARTS, rows, depth // PARTS), BF16),
            V((rows, chan), F32),
            V((rows, chan), F32),
            V((rows, chan), F32),
            V((n // 2 * lb, LANES), BF16),
            V((n // 2 * lb, LANES), F32),
            V((n, lb, LANES), BF16),
            V((n // 2 * lb, LANES), BF16),
            V((rows * NSTATE, LANES), F32),
            V((rows * NSTATE, LANES), F32),
            V((rows, chan), F32),
            V((rows, chan), F32),
            V((rows, chan), F32),
            V((NSTATE, chan), F32),
            V((PARTS * half, LANES), F32),
            V((PARTS, rows // 2, depth // PARTS), F32),
            V((PARTS, rows // 2, depth // PARTS), BF16),
            V((PARTS, rows // 2, depth // PARTS), BF16),
            V((PARTS, half // 2, LANES), F32),
            V((PARTS, half // 2, LANES), BF16),
            V((PARTS, half // 2, LANES), BF16),
            V((PARTS, 2 * outer, part, LANES), F32),
            V((PARTS, 2 * outer, part, LANES), BF16),
            V((PARTS, 2 * outer, part, LANES), BF16),
            V((rows_dev * cq, LANES), F32),
            dma((8,)),
            dma((KSPLIT,)),
            dma((5,)),
            dma((2,)),
            dma((PARTS, 2 * outer)), dma((PARTS, 2 * outer)),
            dma((PARTS,)), dma((PARTS,)),
            dma((PARTS, 2)), dma((PARTS, 2)),
            dma((n,)), dma((n,)),
            dma((n,)), dma((n,)),
            dma((PARTS,)), dma((PARTS,)),
            dma((PARTS,)), dma((PARTS,)),
            dma((PARTS, 2 * outer)), dma((PARTS, 2 * outer)),
        ],
        compiler_params=pltpu.CompilerParams(
            collective_id=0, has_side_effects=True, vmem_limit_bytes=58 * 1024 * 1024
        ),
        name="mixer",
    )(
        hidden, norm_gain[None], conv_weight, conv_offset[None], step_bias[None], log_rates,
        skip_gain[None], live_counts,
        weight, coef_weight.T, step_weight, out_weight, ssm_state, conv_state.transpose(1, 0, 2),
    )
    mixed, new_state, new_conv = pl.pallas_call(
        hand_out,
        out_shape=tuple(jax.ShapeDtypeStruct(a.shape, a.dtype) for a in (mixed, new_state, new_conv)),
        in_specs=[vmem] * 3,
        out_specs=(hbm,) * 3,
        scratch_shapes=[dma((6,))],
        name="hand_out",
    )(*(pltpu.with_memory_space_constraint(v, pltpu.VMEM) for v in (mixed, new_state, new_conv)))
    return mixed, new_state, new_conv.transpose(1, 0, 2)


def solution(mesh):
    in_specs = (
        P(("groups", "weight"), None),
        P(),
        P(None, None, "weight"),
        P(None, "weight"),
        P("weight"),
        P("weight", None),
        P(None, "weight"),
        P("weight"),
        P(None, "weight"),
        P("weight"),
        P("weight", None),
        P("groups", None, "weight"),
        P("groups", None, "weight"),
        P("groups"),
    )
    out_specs = (
        P(("groups", "weight"), None),
        P("groups", None, "weight"),
        P("groups", None, "weight"),
    )
    return jax.shard_map(body, mesh=mesh, in_specs=in_specs, out_specs=out_specs, check_vma=False)
```

```python
import functools

import jax
import jax.numpy as jnp
from jax import lax
from jax.experimental import pallas as pl
from jax.experimental.pallas import tpu as pltpu
from jax.sharding import PartitionSpec as P

NSTATE = 16
DTR = 512
LIVE_MAX = 3
LANES = 128
F32 = jnp.float32
BF16 = jnp.bfloat16
MESH = pl.DeviceIdType.MESH
KSPLIT = 8
PARTS = 4
LOG2E = 1.4426950408889634
SPREAD_IN = 2
SPREAD_OUT = 1
EARLY = 1
AHEAD = 0


def iota(shape, dim):
    return lax.broadcasted_iota(jnp.int32, shape, dim)


def dot(a, b):
    return jnp.dot(a, b, preferred_element_type=F32)


def kernel(
    n, lb,
    hidden_hbm, gain_hbm, convw_hbm, convo_hbm, sbias_hbm, lograte_hbm, skip_hbm, live_hbm,
    w_hbm, coef_hbm, stepw_hbm, outw_hbm, ssm_hbm, conv_hbm,
    mixed, newstate, newconv,
    hidden, gain, convw, convo, sbias, lograte, skip, live,
    raw, perm, wd, coefv, stepv, outv, ssmv, convv,
    xs, xg, xf, lhs, acc, mx, sgate, lowp, lowf, lowr, lowg, inb, outb, step, push, ro, erate,
    pf, mine, s1, r1, k1, s2, r2, k2, s3, r3, fin,
    isem, wsem, lsem, osem, a_s, a_r, b_s, b_r, c_s, c_r, d_s, d_r, e_s, e_r, f_s, f_r, g_s, g_r, h_s, h_r,
):
    me = lax.axis_index("weight")
    core = me % 2
    y = (me // 2) % 2
    z = me // 4
    outer = n // 4
    depth = hidden.shape[1]
    rows_dev = hidden.shape[0]
    ch = depth // LANES
    cq = ch // PARTS
    part = LIVE_MAX * cq
    rows = LIVE_MAX * n
    allrows = rows_dev * n
    chan = wd.shape[2]
    tiles = chan // LANES
    kpart = depth // PARTS
    chunks = (DTR + 2 * NSTATE + LANES - 1) // LANES
    wide = DTR + 2 * NSTATE

    def at(zz, yy, cc):
        return zz * 4 + yy * 2 + cc

    def slab(yy, cc):
        return cc * (2 * outer) + yy * outer

    def device_of(s):
        return at(s % outer, (s // outer) % 2, s // (2 * outer))

    def slot_of(d):
        return slab((d // 2) % 2, d % 2) + d // 4

    ypeer = at(z, 1 - y, core)
    cpeer = at(z, y, 1 - core)
    slot = slab(y, core) + z

    def rdma(src, dst, send, recv, dev):
        return pltpu.make_async_remote_copy(
            src_ref=src, dst_ref=dst, send_sem=send, recv_sem=recv,
            device_id={"weight": dev}, device_id_type=MESH,
        )

    barrier = pltpu.get_barrier_semaphore()
    for k in range(1, n):
        pl.semaphore_signal(barrier, inc=1, device_id={"weight": (me + k) % n}, device_id_type=MESH)

    small = [
        pltpu.make_async_copy(src, dst, isem.at[i])
        for i, (src, dst) in enumerate((
            (hidden_hbm, hidden), (gain_hbm, gain), (convw_hbm, convw), (convo_hbm, convo),
            (sbias_hbm, sbias), (lograte_hbm, lograte), (skip_hbm, skip), (live_hbm, live),
        ))
    ]
    for cp in small:
        cp.start()
    span = raw.shape[0] // KSPLIT

    def w_copy(s):
        at_s = pl.ds(pl.multiple_of(s * span, 256), span)
        return pltpu.make_async_copy(w_hbm.at[at_s], raw.at[at_s], wsem.at[s])

    for s in range(KSPLIT):
        w_copy(s).start()
    conv_cp = pltpu.make_async_copy(conv_hbm, convv, lsem.at[0])
    coef_cp = pltpu.make_async_copy(coef_hbm, coefv.at[pl.ds(0, wide)], lsem.at[1])
    step_cp = pltpu.make_async_copy(stepw_hbm, stepv, lsem.at[2])
    ssm_cp = pltpu.make_async_copy(ssm_hbm, ssmv, lsem.at[3])
    out_cp = pltpu.make_async_copy(outw_hbm, outv, lsem.at[4])
    for cp in (conv_cp, coef_cp, step_cp, ssm_cp, out_cp):
        cp.start()

    small[0].wait()
    small[1].wait()
    h = hidden[...].astype(F32)
    factor = lax.rsqrt(jnp.mean(h * h, axis=-1, keepdims=True) + 1e-05)
    nm = h * factor * gain[...]
    for c in range(ch):
        xs[pl.ds(c // cq * rows_dev * cq + c % cq, rows_dev, stride=cq), :] = nm[:, c * LANES : (c + 1) * LANES]
    for q in range(PARTS):
        xg[q, slot] = xs[pl.ds(q * rows_dev * cq, part), :].astype(BF16)
    coefv[pl.ds(wide, chunks * LANES - wide), :] = jnp.zeros((chunks * LANES - wide, chan), BF16)

    per = 256 // (2 * tiles)
    to, frm = iota((128, 256), 0), iota((128, 256), 1)
    for b in range(2):
        perm[b] = jnp.where(frm == to % per * (2 * tiles) + to // per * 2 + b, 1.0, 0.0).astype(BF16)
    group = span // 256

    def sort_weights(b, first, last):
        @pl.loop(first, last)
        def _(i):
            if b == 0:
                w_copy(i).wait()
            rhs = jnp.concatenate(
                [raw[pl.ds(pl.multiple_of((i * group + g) * 256, 256), 256), :] for g in range(group)], axis=1
            )
            e = dot(perm[b], rhs).astype(BF16)
            for g in range(group):
                at_g = pl.ds(pl.multiple_of((i * group + g) * per, 16), per)
                for j in range(tiles):
                    wd[b, at_g, j * LANES : (j + 1) * LANES] = e[j * per : (j + 1) * per, g * LANES : (g + 1) * LANES]

    sort_weights(0, 0, EARLY)
    pl.semaphore_wait(barrier, n - 1)

    sends = []

    def post(cp):
        cp.start()
        sends.append(cp)

    def settle(count):
        for cp in sends[:count]:
            cp.wait_send()
        del sends[:count]

    def slab_at(q, yy, cc):
        return xg.at[q, pl.ds(slab(yy, cc), outer)]

    hops = [(flip, k) for flip in (1, 0) for k in range(outer) if flip or k]
    relayed = range(PARTS - SPREAD_IN)
    spread = range(PARTS - SPREAD_IN, PARTS)

    def there(flip, k):
        return at((z + k) % outer, (y + flip) % 2, core)

    for q in range(PARTS):
        for flip, k in hops:
            if q in spread or not flip:
                i = flip * outer + k
                post(rdma(xg.at[q, slot], xg.at[q, slot], a_s.at[q, i], a_r.at[q, i], there(flip, k)))

    sort_weights(0, EARLY, KSPLIT)
    sort_weights(1, 0, AHEAD)

    def widen(q, yy, cc):
        first = slab(yy, cc)
        xf[pl.ds(pl.multiple_of((q * n + first) * part, 16), outer * part), :] = (
            xg[q, pl.ds(first, outer)].reshape(outer * part, LANES).astype(F32)
        )

    def arrived(q, flip, k):
        i = flip * outer + k
        src = xg.at[q, slab((y + flip) % 2, core) + (z + outer - k) % outer]
        rdma(src, src, a_s.at[q, i], a_r.at[q, i], ypeer).wait_recv()

    def whole_at(q, cc):
        return xg.at[q, pl.ds(cc * (2 * outer), 2 * outer)]

    def multiply(q):
        for c in range(cq):
            lhs[q, :, c * LANES : (c + 1) * LANES] = xf[
                pl.ds(q * n * part + c, rows, stride=cq), :
            ].astype(BF16)
        return dot(lhs[q], wd[0, pl.ds(q * kpart, kpart), :])

    for q in relayed:
        for k in range(1, outer):
            arrived(q, 0, k)
        src = slab_at(q, y, core)
        post(rdma(src, src, b_s.at[q], b_r.at[q], ypeer))
        post(rdma(src, src, c_s.at[q, 0], c_r.at[q, 0], cpeer))
        widen(q, y, core)
    for q in spread:
        for flip, k in hops:
            arrived(q, flip, k)
        post(rdma(whole_at(q, core), whole_at(q, core), c_s.at[q, 0], c_r.at[q, 0], cpeer))
        widen(q, 0, core)
        widen(q, 1, core)
    for q in relayed:
        src = slab_at(q, y, 1 - core)
        rdma(src, src, c_s.at[q, 0], c_r.at[q, 0], cpeer).wait_recv()
        widen(q, y, 1 - core)

    total = jnp.zeros((rows, chan), F32)

    def relay(q):
        src = slab_at(q, 1 - y, core)
        rdma(src, src, b_s.at[q], b_r.at[q], ypeer).wait_recv()
        post(rdma(src, src, c_s.at[q, 1], c_r.at[q, 1], cpeer))
        widen(q, 1 - y, core)

    waiting = list(relayed)
    for q in spread:
        if waiting:
            relay(waiting.pop(0))
        rdma(whole_at(q, 1 - core), whole_at(q, 1 - core), c_s.at[q, 0], c_r.at[q, 0], cpeer).wait_recv()
        widen(q, 0, 1 - core)
        widen(q, 1, 1 - core)
        total = total + multiply(q)
    for q in relayed:
        if waiting:
            relay(waiting.pop(0))
        src = slab_at(q, 1 - y, 1 - core)
        rdma(src, src, c_s.at[q, 1], c_r.at[q, 1], cpeer).wait_recv()
        widen(q, 1 - y, 1 - core)
        total = total + multiply(q)

    for cp in small[2:]:
        cp.wait()
    conv_cp.wait()
    ci = total.astype(BF16)
    r_at, c_at = iota((rows, allrows), 0), iota((rows, allrows), 1)
    pick = jnp.where(
        c_at == device_of(r_at // LIVE_MAX) * rows_dev + r_at % LIVE_MAX, 1.0, 0.0
    ).astype(BF16)
    total = ci.astype(F32) * convw[pl.ds(3, 1), :] + convo[...]
    for t in range(3):
        total = total + dot(pick, convv[t]) * convw[pl.ds(t, 1), :]
    x = (total / (1.0 + jnp.exp(-total))).astype(BF16)
    mx[...] = x.astype(F32)

    coef_cp.wait()
    low_part = lax.dot_general(x, coefv[...], (((1,), (1,)), ((), ())), preferred_element_type=F32)
    for c in range(chunks):
        lowf[pl.ds(c * rows, rows), :] = low_part[:, c * LANES : (c + 1) * LANES]
        lowp[pl.ds(c * rows, rows), :] = low_part[:, c * LANES : (c + 1) * LANES].astype(BF16)
    if lowp.shape[0] > chunks * rows:
        spare = lowp.shape[0] - chunks * rows
        lowf[pl.ds(chunks * rows, spare), :] = jnp.zeros((spare, LANES), F32)
        lowp[pl.ds(chunks * rows, spare), :] = jnp.zeros((spare, LANES), BF16)

    gathered = len(sends)

    def low_at(ref, d):
        return ref.at[pl.ds(pl.multiple_of(d * lb, 16), lb)]

    count = n // 2
    first_owner = outer // 4 * 4
    mine_low = (me + n - first_owner) % n
    owner = mine_low < count

    def to_owner(k):
        d = first_owner + (me + k) % count
        return rdma(low_at(lowp, d - first_owner), lowr.at[me], d_s.at[k], d_r.at[me], d), d != me

    for k in range(count):
        cp, other = to_owner(k)
        pl.when(other)(cp.start)

    settle(gathered)
    sort_weights(1, AHEAD, KSPLIT)

    def from_owner(k):
        src = low_at(lowg, mine_low % count)
        return rdma(src, src, e_s.at[k], e_r.at[mine_low % count], (me + k) % n)

    @pl.when(owner)
    def _():
        own = low_at(lowf, mine_low % count)[...]
        for k in range(1, n):
            sender = (me + k) % n
            rdma(lowr.at[sender], lowr.at[sender], d_s.at[0], d_r.at[sender], ypeer).wait_recv()
            own = own + lowr[sender].astype(F32)
        low_at(lowg, mine_low % count)[...] = own.astype(BF16)
        for k in range(1, n):
            from_owner(k).start()

    g = jnp.zeros((rows, chan), F32)
    for q in range(PARTS):
        g = g + dot(lhs[q], wd[1, pl.ds(q * kpart, kpart), :])
    sgate[...] = g / (1.0 + jnp.exp(-g))
    erate[...] = jnp.exp(lograte[...]) * (-LOG2E)
    for k in range(count):
        cp, other = to_owner(k)
        pl.when(other)(cp.wait_send)
    row4 = iota((allrows, chan), 0)
    count4 = jnp.zeros((allrows, chan), jnp.int32)
    for m in range(n):
        count4 = jnp.where(row4 // rows_dev == m, live[m], count4)
    alive4 = row4 % rows_dev < count4
    t_at, s_at = iota((allrows, rows), 1), iota((allrows, rows), 0)
    put = jnp.where(
        s_at == device_of(t_at // LIVE_MAX) * rows_dev + t_at % LIVE_MAX, 1.0, 0.0
    ).astype(BF16)
    for t in range(3):
        new = convv[t + 1].astype(F32) if t < 2 else dot(put, ci)
        newconv[t] = jnp.where(alive4, new, convv[t].astype(F32)).astype(BF16)
    step_cp.wait()
    ssm_cp.wait()

    @pl.loop(0, n)
    def _(m):
        newstate[m * rows_dev + LIVE_MAX] = ssmv[m * rows_dev + LIVE_MAX]


    for o in range(count):
        src = low_at(lowg, o)
        cp = rdma(src, src, e_s.at[0], e_r.at[o], ypeer)
        pl.when(first_owner + o != me)(cp.wait_recv)

    low = jnp.concatenate([lowg[pl.ds(c * rows, rows), :] for c in range(DTR // LANES)], axis=1)
    v = dot(low, stepv[...]) + sbias[...]
    step[...] = jnp.maximum(v, 0.0) + jnp.log1p(jnp.exp(-jnp.abs(v)))
    push[...] = step[...] * mx[...]
    coefs = lowg[pl.ds(DTR // LANES * rows, rows), :].astype(F32)
    for q in range(NSTATE):
        inb[pl.ds(q, rows, stride=NSTATE), :] = jnp.broadcast_to(coefs[:, q : q + 1], (rows, LANES))
        outb[pl.ds(q, rows, stride=NSTATE), :] = jnp.broadcast_to(
            coefs[:, NSTATE + q : NSTATE + q + 1], (rows, LANES)
        )

    @pl.loop(0, n, unroll=4)
    def _(m):
        alive = live[m]
        for j in range(LIVE_MAX):
            r = slot_of(m) * LIVE_MAX + j
            old = ssmv[m * rows_dev + j].astype(F32)
            st = step[pl.ds(r, 1), :]
            sx = push[pl.ds(r, 1), :]
            at_r = pl.ds(pl.multiple_of(r * NSTATE, NSTATE), NSTATE)
            inc = jnp.concatenate([inb[at_r, :]] * tiles, axis=1)
            outc = jnp.concatenate([outb[at_r, :]] * tiles, axis=1)
            upd = jnp.exp2(st * erate[...]) * old + inc * sx
            ro[pl.ds(r, 1), :] = jnp.sum(outc * upd, axis=0, keepdims=True)
            keep = jnp.full(old.shape, alive, jnp.int32) > j
            newstate[m * rows_dev + j] = jnp.where(keep, upd, old).astype(BF16)


    row3 = iota((rows, chan), 0)
    count3 = jnp.zeros((rows, chan), jnp.int32)
    for m in range(n):
        count3 = jnp.where(row3 // LIVE_MAX == slot_of(m), live[m], count3)
    read = (ro[...] + skip[...] * mx[...]) * sgate[...]
    gated = jnp.where(row3 % LIVE_MAX < count3, read, 0.0).astype(BF16)

    out_cp.wait()
    half = rows * cq // 2
    quarter = half // 2

    def project(u):
        p = dot(gated, outv[:, pl.ds(u * kpart, kpart)])
        low_half, high_half = p[: rows // 2], p[rows // 2 :]
        first = jnp.full(low_half.shape, core, jnp.int32) == 0
        s1[u] = jnp.where(first, high_half, low_half).astype(BF16)
        post(rdma(s1.at[u], r1.at[u], f_s.at[u], f_r.at[u], cpeer))
        mine[u] = jnp.where(first, low_half, high_half)

    sent_by_y = range(PARTS - SPREAD_OUT)

    def add_core(u):
        rdma(r1.at[u], r1.at[u], f_s.at[u], f_r.at[u], cpeer).wait_recv()
        base = u * half
        both = mine[u] + r1[u].astype(F32)
        for i in range(cq):
            pf[pl.ds(base + i, rows // 2, stride=cq), :] = both[:, i * LANES : (i + 1) * LANES]
        if u in sent_by_y:
            far = pl.multiple_of((1 - y) * quarter, 16)
            near = pl.multiple_of(y * quarter, 16)
            s2[u] = pf[pl.ds(base + far, quarter), :].astype(BF16)
            post(rdma(s2.at[u], r2.at[u], g_s.at[u], g_r.at[u], ypeer))
            k1[u] = pf[pl.ds(base + near, quarter), :]
        else:
            both = pf[pl.ds(base, half), :]
            s3[u] = both.astype(BF16).reshape(2 * outer, part, LANES)
            k2[u] = both.reshape(2 * outer, part, LANES)
            for flip, k in hops:
                i = flip * outer + k
                block = (y + flip) % 2 * outer + (z + k) % outer
                post(rdma(s3.at[u, block], r3.at[u, i], h_s.at[u, i], h_r.at[u, i], there(flip, k)))

    def add_y(u):
        rdma(r2.at[u], r2.at[u], g_s.at[u], g_r.at[u], ypeer).wait_recv()
        both = k1[u] + r2[u].astype(F32)
        s3[u, pl.ds(0, outer)] = both.astype(BF16).reshape(outer, part, LANES)
        k2[u, pl.ds(0, outer)] = both.reshape(outer, part, LANES)
        for k in range(1, outer):
            post(rdma(s3.at[u, (z + k) % outer], r3.at[u, k], h_s.at[u, k], h_r.at[u, k], there(0, k)))

    fin[pl.ds(part, rows_dev * cq - part), :] = jnp.zeros((rows_dev * cq - part, LANES), F32)

    def finish(u):
        both = k2[u, z if u in sent_by_y else y * outer + z]
        for flip, k in hops:
            if u in sent_by_y and flip:
                continue
            i = flip * outer + k
            rdma(r3.at[u, i], r3.at[u, i], h_s.at[u, i], h_r.at[u, i], ypeer).wait_recv()
            both = both + r3[u, i].astype(F32)
        fin[pl.ds(0, part), :] = both
        for c in range(cq):
            cols = slice((u * cq + c) * LANES, (u * cq + c + 1) * LANES)
            mixed[:, cols] = (hidden[:, cols].astype(F32) + fin[pl.ds(c, rows_dev, stride=cq), :]).astype(BF16)

    summed = len(sends)
    for u in range(PARTS):
        project(u)
        if u:
            add_core(u - 1)
    add_core(PARTS - 1)
    settle(summed)

    @pl.when(owner)
    def _():
        for k in range(1, n):
            from_owner(k).wait_send()

    for u in sent_by_y:
        add_y(u)
    settle(len(sends) - (outer - 1))
    for u in [u for u in range(PARTS) if u not in sent_by_y] + list(sent_by_y):
        finish(u)
    for cp in sends:
        cp.wait_send()


def hand_out(mixed, state, conv, mixed_out, state_out, conv_out, sem):
    step = state.shape[0] // 4
    trips = [(state.at[pl.ds(i * step, step)], state_out.at[pl.ds(i * step, step)]) for i in range(4)]
    trips += [(conv, conv_out), (mixed, mixed_out)]
    copies = [pltpu.make_async_copy(a, o, sem.at[i]) for i, (a, o) in enumerate(trips)]
    for cp in copies:
        cp.start()
    for cp in copies:
        cp.wait()


def body(
    hidden, norm_gain, in_weight, conv_weight, conv_offset, coef_weight, step_weight,
    step_bias, log_rates, skip_gain, out_weight, ssm_state, conv_state, live_counts,
):
    n = lax.axis_size("weight")
    rows_dev, depth = hidden.shape
    chan = in_weight.shape[2]
    tiles = chan // LANES
    ch = depth // LANES
    rows = LIVE_MAX * n
    allrows = rows_dev * n
    outer = n // 4
    chunks = (DTR + 2 * NSTATE + LANES - 1) // LANES
    lb = -(-(chunks * rows) // (8 * n)) * 16
    cq = ch // PARTS
    part = LIVE_MAX * cq
    half = rows * cq // 2
    weight = in_weight.reshape(depth, 2, tiles, LANES).transpose(0, 2, 1, 3).reshape(depth * tiles * 2, LANES)
    vmem = pl.BlockSpec(memory_space=pltpu.VMEM)
    hbm = pl.BlockSpec(memory_space=pl.ANY)
    dma = pltpu.SemaphoreType.DMA
    V = pltpu.VMEM
    mixed, new_state, new_conv = pl.pallas_call(
        functools.partial(kernel, n, lb),
        out_shape=(
            V(hidden.shape, BF16),
            V(ssm_state.shape, BF16),
            V((3, allrows, chan), BF16),
        ),
        in_specs=[hbm] * 14,
        out_specs=(vmem,) * 3,
        scratch_shapes=[
            V(hidden.shape, BF16),
            V((1, depth), F32),
            V(conv_weight.shape, F32),
            V((1, chan), F32),
            V((1, chan), F32),
            V(log_rates.shape, F32),
            V((1, chan), F32),
            pltpu.SMEM(live_counts.shape, jnp.int32),
            V(weight.shape, BF16),
            V((2, 128, 256), BF16),
            V((2, depth, chan), BF16),
            V((chunks * LANES, chan), BF16),
            V(step_weight.shape, BF16),
            V(out_weight.shape, BF16),
            V(ssm_state.shape, BF16),
            V((3, allrows, chan), BF16),
            V((rows_dev * ch, LANES), F32),
            V((PARTS, n, part, LANES), BF16),
            V((PARTS * n * part, LANES), F32),
            V((PARTS, rows, depth // PARTS), BF16),
            V((rows, chan), F32),
            V((rows, chan), F32),
            V((rows, chan), F32),
            V((n // 2 * lb, LANES), BF16),
            V((n // 2 * lb, LANES), F32),
            V((n, lb, LANES), BF16),
            V((n // 2 * lb, LANES), BF16),
            V((rows * NSTATE, LANES), F32),
            V((rows * NSTATE, LANES), F32),
            V((rows, chan), F32),
            V((rows, chan), F32),
            V((rows, chan), F32),
            V((NSTATE, chan), F32),
            V((PARTS * half, LANES), F32),
            V((PARTS, rows // 2, depth // PARTS), F32),
            V((PARTS, rows // 2, depth // PARTS), BF16),
            V((PARTS, rows // 2, depth // PARTS), BF16),
            V((PARTS, half // 2, LANES), F32),
            V((PARTS, half // 2, LANES), BF16),
            V((PARTS, half // 2, LANES), BF16),
            V((PARTS, 2 * outer, part, LANES), F32),
            V((PARTS, 2 * outer, part, LANES), BF16),
            V((PARTS, 2 * outer, part, LANES), BF16),
            V((rows_dev * cq, LANES), F32),
            dma((8,)),
            dma((KSPLIT,)),
            dma((5,)),
            dma((2,)),
            dma((PARTS, 2 * outer)), dma((PARTS, 2 * outer)),
            dma((PARTS,)), dma((PARTS,)),
            dma((PARTS, 2)), dma((PARTS, 2)),
            dma((n,)), dma((n,)),
            dma((n,)), dma((n,)),
            dma((PARTS,)), dma((PARTS,)),
            dma((PARTS,)), dma((PARTS,)),
            dma((PARTS, 2 * outer)), dma((PARTS, 2 * outer)),
        ],
        compiler_params=pltpu.CompilerParams(
            collective_id=0, has_side_effects=True, vmem_limit_bytes=58 * 1024 * 1024
        ),
        name="mixer",
    )(
        hidden, norm_gain[None], conv_weight, conv_offset[None], step_bias[None], log_rates,
        skip_gain[None], live_counts,
        weight, coef_weight.T, step_weight, out_weight, ssm_state, conv_state.transpose(1, 0, 2),
    )
    mixed, new_state, new_conv = pl.pallas_call(
        hand_out,
        out_shape=tuple(jax.ShapeDtypeStruct(a.shape, a.dtype) for a in (mixed, new_state, new_conv)),
        in_specs=[vmem] * 3,
        out_specs=(hbm,) * 3,
        scratch_shapes=[dma((6,))],
        name="hand_out",
    )(*(pltpu.with_memory_space_constraint(v, pltpu.VMEM) for v in (mixed, new_state, new_conv)))
    return mixed, new_state, new_conv.transpose(1, 0, 2)


def solution(mesh):
    in_specs = (
        P(("groups", "weight"), None),
        P(),
        P(None, None, "weight"),
        P(None, "weight"),
        P("weight"),
        P("weight", None),
        P(None, "weight"),
        P("weight"),
        P(None, "weight"),
        P("weight"),
        P("weight", None),
        P("groups", None, "weight"),
        P("groups", None, "weight"),
        P("groups"),
    )
    out_specs = (
        P(("groups", "weight"), None),
        P("groups", None, "weight"),
        P("groups", None, "weight"),
    )
    return jax.shard_map(body, mesh=mesh, in_specs=in_specs, out_specs=out_specs, check_vma=False)
```
